256 devices in a mesh: grp: 16 (over z_lo, x, core), mem: 16 (over y, z_hi).
Axes of the slice: x: 4, y: 4, z: 8 (z_hi: 4, z_lo: 2; z = z_hi * 2 + z_lo), core: 2. Of those that a mesh axis runs over, the one named last changes fastest.
Arguments:
- rhs: float32 [384, 896, 384], P('grp', 'mem'), may hold values from -6 to 6
- conductivity: float32 [384, 896], P('grp', 'mem'), may hold values from 0.2 to 5
- local_inverse: bfloat16 [524288, 2048], P(('grp', 'mem')), may hold values from -0.125 to 0.125
- coarse_basis: float32 [384, 896, 16], P('grp', 'mem'), may hold values from -0.5 to 0.5
- coarse_inverse: float32 [4096, 4096], P(('grp', 'mem')), may hold values from -3 to 8, as said below
Outputs:
- solution: float32 [384, 896, 384], P('grp', 'mem')
The draws below stay inside these ranges and needn't reach their ends.
Inputs may be any that keep to these rules, and one draw needn't show every extreme that they name: coarse_inverse is symmetric up to rounding, with a positive diagonal.
All inputs are finite; a program needn't handle non-finite values.
Results may differ from the reference program's by a relative error of at most 0.0005.
Values may be sent and summed in bfloat16 or wider, within the bound.
A program may use at most 128 MiB of HBM per device.

```python
import math
import jax
import jax.numpy as jnp
from jax import lax

OX = 24
OY = 56
OV = 4
MODES = 16
RHS = 384
ITERS = 2
LOC = 2048
NC = 4096
NX = 384
NY = 896
N_GRP = 16
N_MEM = 16


def draw_coarse_inverse(key, part):
    base = jax.random.normal(jax.random.fold_in(key, 11), (NC, NC), jnp.float32) * (0.5 / math.sqrt(NC))
    symmetric = base + base.T + jnp.eye(NC, dtype=jnp.float32)
    return symmetric


def block_levels(rng, dims, cuts, smallest, high):
    loudness, own = 1.0, jax.random.fold_in(rng, 6)
    for dim, blocks in cuts:
        heights = jnp.exp(jax.random.uniform(jax.random.fold_in(own, dim), (blocks,), jnp.float32, smallest / len(cuts), high / len(cuts)))
        loudness = loudness * jnp.repeat(heights, dims[dim] // blocks).reshape([-1 if axis == dim else 1 for axis in range(len(dims))])
    return loudness


def scatter_about(stream_key, dims, width, reach, shards=(), kind=jnp.bfloat16):
    loudness = block_levels(stream_key, dims, shards, -0.22, 0.18) if shards else 1.0
    entries = jax.random.normal(stream_key, dims, jnp.float32) * width * loudness
    return jnp.minimum(jnp.maximum(entries, -reach), reach).astype(kind)


def setup_inputs(seed: int = 0) -> dict:
    arg_keys = jax.random.split(jax.random.key(seed), 6)
    rhs = scatter_about(arg_keys[0], (NX, NY, RHS), 1.0, 6.0, ((0, 16), (1, 16)), jnp.float32)
    conductivity = jnp.clip(jnp.exp(math.log(5.0) - 3.218876 * jax.random.uniform(arg_keys[1], (NX, NY), jnp.float32) ** block_levels(arg_keys[1], (NX, NY), ((0, 16), (1, 16)), -0.2, 0.2)), 0.2, 5.0)
    local_inverse = scatter_about(arg_keys[2], (N_GRP * N_MEM * LOC, LOC), LOC ** -0.5, 0.125, ((0, 256),))
    coarse_basis = scatter_about(arg_keys[3], (NX, NY, MODES), (OX * OY // 8) ** -0.5, 0.5, ((0, 16), (1, 16)), jnp.float32)
    coarse_inverse = draw_coarse_inverse(jax.random.fold_in(arg_keys[5], 71), 0)
    return dict(rhs=rhs, conductivity=conductivity, local_inverse=local_inverse, coarse_basis=coarse_basis, coarse_inverse=coarse_inverse)


def apply_operator(field_pad, conduct_pad):
    center = field_pad[1:-1, 1:-1]
    conduct_mid = conduct_pad[1:-1, 1:-1]
    neighbour_fields = (field_pad[2:, 1:-1], field_pad[:-2, 1:-1], field_pad[1:-1, 2:], field_pad[1:-1, :-2])
    neighbour_conduct = (conduct_pad[2:, 1:-1], conduct_pad[:-2, 1:-1], conduct_pad[1:-1, 2:], conduct_pad[1:-1, :-2])
    summed = jnp.zeros(center.shape, jnp.float32)
    for other_field, other_conduct in zip(neighbour_fields, neighbour_conduct):
        face = 0.5 * (conduct_mid + other_conduct)
        summed = summed + face[:, :, None] * (center - other_field)
    return summed


def reference(rhs, conductivity, local_inverse, coarse_basis, coarse_inverse):
    groups = N_GRP
    members = N_MEM
    span_x = OX + 2 * OV
    span_y = OY + 2 * OV
    conduct_pad = jnp.pad(conductivity, 1)
    solution = jnp.zeros(rhs.shape, jnp.float32)
    basis_five = coarse_basis.reshape(groups, OX, members, OY, MODES)
    for sweep in range(ITERS):
        solution_pad = jnp.pad(solution, ((1, 1), (1, 1), (0, 0)))
        residual = rhs - apply_operator(solution_pad, conduct_pad)
        residual_pad = jnp.pad(residual, ((OV, OV), (OV, OV), (0, 0)))

        def local_solve(subdomain):
            group_index = subdomain // members
            member_index = subdomain % members
            zero_start = jnp.zeros((), jnp.int32)
            extended = lax.dynamic_slice(residual_pad, (group_index * OX, member_index * OY, zero_start), (span_x, span_y, RHS))
            flat_rows = extended.reshape(LOC, RHS).astype(jnp.bfloat16)
            inverse_block = lax.dynamic_slice_in_dim(local_inverse, subdomain * LOC, LOC, 0)
            product = jnp.dot(inverse_block, flat_rows, preferred_element_type=jnp.float32)
            return product.reshape(span_x, span_y, RHS)[OV:OV + OX, OV:OV + OY]

        fine_blocks = lax.map(local_solve, jnp.arange(groups * members, dtype=jnp.int32))
        fine_part = fine_blocks.reshape(groups, members, OX, OY, RHS).transpose(0, 2, 1, 3, 4).reshape(NX, NY, RHS)
        residual_five = residual.reshape(groups, OX, members, OY, RHS)
        restricted = jnp.einsum('gxmyk,gxmyr->gmkr', basis_five, residual_five, precision=lax.Precision.HIGHEST).reshape(NC, RHS)
        lifted = jnp.dot(coarse_inverse, restricted, precision=lax.Precision.HIGHEST, preferred_element_type=jnp.float32)
        lifted = lifted.reshape(groups, members, MODES, RHS)
        coarse_part = jnp.einsum('gxmyk,gmkr->gxmyr', basis_five, lifted, precision=lax.Precision.HIGHEST).reshape(NX, NY, RHS)
        solution = solution + fine_part + coarse_part
    return solution
```

```python
import functools
import jax
import jax.numpy as jnp
from jax import lax
from jax.experimental import pallas as pl
from jax.experimental.pallas import tpu as pltpu
from jax.sharding import PartitionSpec as P

OV = 4
NZ = 4
MESH = pl.DeviceIdType.MESH
F32 = jnp.float32
BF16 = jnp.bfloat16


def split(v):
    hi = v.astype(BF16)
    lo = (v - hi.astype(F32)).astype(BF16)
    return hi, lo


def dot(a, b):
    return jnp.dot(a, b, preferred_element_type=F32)


def kernel(
    n_grp, n_mem, own_x, own_y,
    rhs_hbm, cond, linv_hbm, basis_t, cinv_hbm,
    out_hbm,
    lbuf, res, win, fine, sol, outbuf, cpad, facex, facey,
    bres, bcor, rblk, cblk, csplit, part, qbuf,
    ysend, yrecv, esend, erecv, condrecv,
    in_sem, out_sem, cloc_sem,
    c_send, c_recv, cond_send, cond_recv,
    az_send, az_recv, ay_send, ay_recv, rs_send, rs_recv,
    yh_send, yh_recv, xh_send, xh_recv, ex_send, ex_recv,
):
    g = lax.axis_index("grp")
    m = lax.axis_index("mem")
    n_y = n_mem // NZ
    my = m // NZ
    mz = lax.rem(m, NZ)
    span_y = own_y + 2 * OV
    columns = rhs_hbm.shape[2]
    modes = basis_t.shape[1]
    edge = OV * span_y
    mid = own_x * span_y
    g_up = lax.rem(g + 1, n_grp)
    g_dn = lax.rem(g + n_grp - 1, n_grp)
    m_up = lax.rem(m + 1, n_mem)
    m_dn = lax.rem(m + n_mem - 1, n_mem)

    def z_peer(d):
        return my * NZ + lax.rem(mz + d, NZ)

    def y_peer(d):
        return lax.rem(my + d, n_y) * NZ + mz

    load_rhs = pltpu.make_async_copy(rhs_hbm, res.at[0, :, pl.ds(8, own_y), :], in_sem.at[0])
    load_inv = pltpu.make_async_copy(linv_hbm.at[pl.ds(edge, mid), :], lbuf, in_sem.at[1])
    load_rhs.start()
    load_inv.start()

    barrier = pltpu.get_barrier_semaphore()

    def greet_grp(d, carry):
        pl.semaphore_signal(
            barrier, inc=1, device_id={"grp": lax.rem(g + d, n_grp)}, device_id_type=MESH
        )
        return carry

    lax.fori_loop(1, n_grp, greet_grp, 0)
    greets = n_grp - 1
    for peer in [z_peer(d) for d in range(1, NZ)] + [y_peer(d) for d in range(1, n_y)] + [m_up, m_dn]:
        pl.semaphore_signal(barrier, inc=1, device_id={"mem": peer}, device_id_type=MESH)
        greets += 1

    def prepare_basis(i, carry):
        wide = jnp.concatenate([basis_t[2 * i], basis_t[2 * i + 1]], axis=1)
        hi, lo = split(wide)
        bres[i] = jnp.concatenate([hi, lo], axis=0)
        tall = jnp.concatenate([hi.astype(F32), lo.astype(F32), hi.astype(F32)], axis=0)
        bcor[i] = jnp.transpose(tall).astype(BF16)
        return carry

    lax.fori_loop(0, own_x // 2, prepare_basis, 0)

    own_rows = pl.ds(pl.multiple_of(m * modes, modes), modes)

    def restrict(it):
        def step(i, total):
            pair = res[it, pl.ds(2 * i, 2), pl.ds(8, own_y), :].reshape(2 * own_y, columns)
            hi, lo = split(pair)
            both = dot(bres[i], hi)
            return total + both[:modes] + both[modes:] + dot(bres[i, pl.ds(0, modes), :], lo)

        total = lax.fori_loop(0, own_x // 2, step, jnp.zeros((modes, columns), F32))
        rblk[it, own_rows, :] = total

    low_half = lax.broadcasted_iota(jnp.int32, (own_x // 2, 8, columns), 1) < OV

    def flip(v):
        return pltpu.roll(v, OV, 1)

    def pack_y(it):
        left = res[it, :, pl.ds(8, 8), :].reshape(own_x // 2, 2, 8, columns)
        right = res[it, :, pl.ds(own_y, 8), :].reshape(own_x // 2, 2, 8, columns)
        lo_side = jnp.where(low_half, left[:, 0], flip(left[:, 1]))
        hi_side = jnp.where(low_half, flip(right[:, 0]), right[:, 1])
        ysend[it, 0] = lo_side.reshape(own_x * OV, columns).astype(BF16)
        ysend[it, 1] = hi_side.reshape(own_x * OV, columns).astype(BF16)

    def y_copy(it, side):
        return pltpu.make_async_remote_copy(
            src_ref=ysend.at[it, side],
            dst_ref=yrecv.at[it, 1 - side],
            send_sem=yh_send.at[it, side],
            recv_sem=yh_recv.at[it, 1 - side],
            device_id={"mem": m_dn if side == 0 else m_up},
            device_id_type=MESH,
        )

    def y_wait(it, side):
        pltpu.make_async_remote_copy(
            src_ref=ysend.at[it, side], dst_ref=yrecv.at[it, side],
            send_sem=yh_send.at[it, side], recv_sem=yh_recv.at[it, side],
            device_id={"mem": m_dn if side == 0 else m_up}, device_id_type=MESH,
        ).wait_recv()

    def unpack_y(it):
        low = jnp.where(m == 0, 0.0, yrecv[it, 0].astype(F32)).reshape(own_x // 2, 8, columns)
        high = jnp.where(m == n_mem - 1, 0.0, yrecv[it, 1].astype(F32)).reshape(own_x // 2, 8, columns)
        low_even, high_odd = flip(low), flip(high)
        for i in range(own_x // 2):
            res[it, 2 * i, pl.ds(0, 8), :] = low_even[i]
            res[it, 2 * i + 1, pl.ds(0, 8), :] = low[i]
            res[it, 2 * i, pl.ds(own_y + 8, 8), :] = high[i]
            res[it, 2 * i + 1, pl.ds(own_y + 8, 8), :] = high_odd[i]

    def assemble(it):
        def row(x, carry):
            start = pl.multiple_of((x + OV) * span_y, span_y)
            win[it, pl.ds(start, span_y), :] = res[it, x, pl.ds(8 - OV, span_y), :].astype(BF16)
            return carry

        lax.fori_loop(0, own_x, row, 0)

    def x_copy(it, side):
        src = edge if side == 0 else mid
        dst = edge + mid if side == 0 else 0
        return pltpu.make_async_remote_copy(
            src_ref=win.at[it, pl.ds(src, edge), :],
            dst_ref=win.at[it, pl.ds(dst, edge), :],
            send_sem=xh_send.at[it, side],
            recv_sem=xh_recv.at[it, 1 - side],
            device_id={"grp": g_dn if side == 0 else g_up},
            device_id_type=MESH,
        )

    def x_wait(it, side):
        dst = 0 if side == 0 else edge + mid
        pltpu.make_async_remote_copy(
            src_ref=win.at[it, pl.ds(dst, edge), :],
            dst_ref=win.at[it, pl.ds(dst, edge), :],
            send_sem=xh_send.at[it, side],
            recv_sem=xh_recv.at[it, side],
            device_id={"grp": g_dn if side == 0 else g_up},
            device_id_type=MESH,
        ).wait_recv()

    def finish_x(it):
        x_wait(it, 0)
        x_wait(it, 1)

        @pl.when(g == 0)
        def _():
            win[it, pl.ds(0, edge), :] = jnp.zeros((edge, columns), BF16)

        @pl.when(g == n_grp - 1)
        def _():
            win[it, pl.ds(edge + mid, edge), :] = jnp.zeros((edge, columns), BF16)

    chunk = OV * span_y

    def fine_mid(it):
        def step(i, carry):
            rows = pl.ds(pl.multiple_of(i * chunk, chunk), chunk)
            got = dot(lbuf[rows, pl.ds(edge, mid)], win[it, pl.ds(edge, mid), :])
            fine[pl.ds(i * OV, OV)] = got.reshape(OV, span_y, columns)
            return carry

        lax.fori_loop(0, own_x // OV, step, 0)

    def fine_edge(it):
        def step(i, carry):
            rows = pl.ds(pl.multiple_of(i * chunk, chunk), chunk)
            got = dot(lbuf[rows, pl.ds(0, edge)], win[it, pl.ds(0, edge), :])
            got += dot(lbuf[rows, pl.ds(edge + mid, edge)], win[it, pl.ds(edge + mid, edge), :])
            fine[pl.ds(i * OV, OV)] += got.reshape(OV, span_y, columns)
            return carry

        lax.fori_loop(0, own_x // OV, step, 0)

    def z_copy(it, d):
        return pltpu.make_async_remote_copy(
            src_ref=rblk.at[it, own_rows, :], dst_ref=rblk.at[it, own_rows, :],
            send_sem=az_send.at[it, d], recv_sem=az_recv.at[it, d],
            device_id={"mem": z_peer(d)}, device_id_type=MESH,
        )

    def y_forward(it, d, src_d):
        block = my * NZ + lax.rem(mz + NZ - src_d, NZ)
        rows = pl.ds(pl.multiple_of(block * modes, modes), modes)
        return pltpu.make_async_remote_copy(
            src_ref=rblk.at[it, rows, :], dst_ref=rblk.at[it, rows, :],
            send_sem=ay_send.at[it, d, src_d], recv_sem=ay_recv.at[it, d, src_d],
            device_id={"mem": y_peer(d)}, device_id_type=MESH,
        )

    def gather_start(it):
        for d in range(1, NZ):
            z_copy(it, d).start()
        for d in range(1, n_y):
            y_forward(it, d, 0).start()

    def gather_forward(it):
        for src_d in (1, 3, 2):
            z_copy(it, src_d).wait_recv()
            for d in range(1, n_y):
                y_forward(it, d, src_d).start()

    def gather_finish(it):
        for src_d in range(NZ):
            for d in range(1, n_y):
                y_forward(it, d, src_d).wait_recv()

    def c_copy(d):
        dest = lax.rem(g + d, n_grp)
        return pltpu.make_async_remote_copy(
            src_ref=cinv_hbm.at[:, pl.ds(pl.multiple_of(dest * n_mem * modes, n_mem * modes), n_mem * modes)],
            dst_ref=cblk.at[pl.ds(pl.multiple_of(g * modes, modes), modes), :],
            send_sem=c_send.at[d], recv_sem=c_recv.at[d],
            device_id={"grp": dest}, device_id_type=MESH,
        )

    c_local = pltpu.make_async_copy(
        cinv_hbm.at[:, pl.ds(pl.multiple_of(g * n_mem * modes, n_mem * modes), n_mem * modes)],
        cblk.at[pl.ds(pl.multiple_of(g * modes, modes), modes), :],
        cloc_sem,
    )

    def each_grp(action):
        def body(d, carry):
            action(d)
            return carry

        lax.fori_loop(1, n_grp, body, 0)

    def coarse_multiply(it):
        hi, lo = split(rblk[it])

        def step(i, carry):
            rows = pl.ds(pl.multiple_of(i * 64, 64), 64)
            c_hi, c_lo = csplit[0, rows, :], csplit[1, rows, :]
            part[it, rows, :] = dot(c_hi, hi) + (dot(c_hi, lo) + dot(c_lo, hi))
            return carry

        lax.fori_loop(0, n_grp * modes // 64, step, 0)

    def rs_copy(it, d):
        dest = lax.rem(g + d, n_grp)
        return pltpu.make_async_remote_copy(
            src_ref=part.at[it, pl.ds(pl.multiple_of(dest * modes, modes), modes), :],
            dst_ref=qbuf.at[it, d],
            send_sem=rs_send.at[it, d], recv_sem=rs_recv.at[it, d],
            device_id={"grp": dest}, device_id_type=MESH,
        )

    def lift(it):
        each_grp(lambda d: rs_copy(it, d).wait_recv())

        def add(d, total):
            return total + qbuf[it, d]

        own = part[it, pl.ds(pl.multiple_of(g * modes, modes), modes), :]
        lifted = lax.fori_loop(1, n_grp, add, own)
        hi, lo = split(lifted)
        return jnp.concatenate([hi.astype(F32), hi.astype(F32), lo.astype(F32)], axis=0).astype(BF16)

    def cond_copy(slot):
        if slot < 2:
            device = {"grp": g_up if slot == 0 else g_dn}
        else:
            device = {"mem": m_up if slot == 2 else m_dn}
        return pltpu.make_async_remote_copy(
            src_ref=cond, dst_ref=condrecv.at[slot],
            send_sem=cond_send.at[slot], recv_sem=cond_recv.at[slot],
            device_id=device, device_id_type=MESH,
        )

    def make_faces():
        for slot in range(4):
            cond_copy(slot).wait_recv()
        shape = (own_y, own_y)
        eye = lax.broadcasted_iota(jnp.int32, shape, 0) == lax.broadcasted_iota(jnp.int32, shape, 1)
        lane = lax.broadcasted_iota(jnp.int32, (1, own_y), 1)

        def spread(row):
            full = jnp.where(eye, jnp.broadcast_to(row, shape), 0.0)
            return jnp.broadcast_to(jnp.sum(full, axis=1, keepdims=True), (own_y, 128))

        def pick(row, at):
            one = jnp.sum(jnp.where(lane == at, row, 0.0), axis=1, keepdims=True)
            return jnp.broadcast_to(one, (8, 128))

        def row_of(x, carry):
            cpad[x + 1, pl.ds(8, own_y), :] = spread(cond[pl.ds(x, 1), :])
            low = jnp.where(m == 0, 0.0, pick(condrecv[2, pl.ds(x, 1), :], own_y - 1))
            high = jnp.where(m == n_mem - 1, 0.0, pick(condrecv[3, pl.ds(x, 1), :], 0))
            cpad[x + 1, pl.ds(0, 8), :] = low
            cpad[x + 1, pl.ds(own_y + 8, 8), :] = high
            return carry

        lax.fori_loop(0, own_x, row_of, 0)
        first = jnp.where(g == 0, 0.0, condrecv[0, pl.ds(own_x - 1, 1), :])
        last = jnp.where(g == n_grp - 1, 0.0, condrecv[1, pl.ds(0, 1), :])
        cpad[0, pl.ds(8, own_y), :] = spread(first)
        cpad[own_x + 1, pl.ds(8, own_y), :] = spread(last)

        def face_x(x, carry):
            facex[x] = 0.5 * (cpad[x, pl.ds(8, own_y), :] + cpad[x + 1, pl.ds(8, own_y), :])
            return carry

        def face_y(x, carry):
            facey[x] = 0.5 * (cpad[x + 1, pl.ds(7, own_y + 8), :] + cpad[x + 1, pl.ds(8, own_y + 8), :])
            return carry

        lax.fori_loop(0, own_x + 1, face_x, 0)
        lax.fori_loop(0, own_x, face_y, 0)

    def ex_copy(side):
        if side < 2:
            src = sol.at[1 if side == 0 else own_x, pl.ds(8, own_y), :]
            dst = sol.at[own_x + 1 if side == 0 else 0, pl.ds(8, own_y), :]
            device = {"grp": g_dn if side == 0 else g_up}
        else:
            src = esend.at[side - 2]
            dst = erecv.at[side - 2]
            device = {"mem": m_dn if side == 2 else m_up}
        return pltpu.make_async_remote_copy(
            src_ref=src, dst_ref=dst, send_sem=ex_send.at[side], recv_sem=ex_recv.at[side],
            device_id=device, device_id_type=MESH,
        )

    def correct_first(lifted):
        def step(i, carry):
            co = dot(bcor[i], lifted)
            for j in range(2):
                value = fine[2 * i + j, pl.ds(OV, own_y), :] + co[j * own_y : (j + 1) * own_y]
                sol[2 * i + j + 1, pl.ds(8, own_y), :] = value
                esend[0, pl.ds(2 * i + j, 1), :] = value[:1]
                esend[1, pl.ds(2 * i + j, 1), :] = value[own_y - 1 :]
            return carry

        lax.fori_loop(0, own_x // 2, step, 0)

    def finish_sol():
        for side in range(4):
            ex_copy(side).wait_recv()

        @pl.when(g == 0)
        def _():
            sol[0, pl.ds(8, own_y), :] = jnp.zeros((own_y, columns), F32)

        @pl.when(g == n_grp - 1)
        def _():
            sol[own_x + 1, pl.ds(8, own_y), :] = jnp.zeros((own_y, columns), F32)

        def row(x, carry):
            high = jnp.where(m == n_mem - 1, 0.0, erecv[0, pl.ds(x, 1), :])
            low = jnp.where(m == 0, 0.0, erecv[1, pl.ds(x, 1), :])
            sol[x + 1, pl.ds(7, 1), :] = low
            sol[x + 1, pl.ds(own_y + 8, 1), :] = high
            return carry

        lax.fori_loop(0, own_x, row, 0)

    def thrice(v):
        return jnp.concatenate([v] * (columns // 128), axis=1)

    def second_residual():
        def row(x, carry):
            c = sol[x + 1, pl.ds(8, own_y), :]
            total = thrice(facex[x + 1]) * (c - sol[x + 2, pl.ds(8, own_y), :])
            total += thrice(facex[x]) * (c - sol[x, pl.ds(8, own_y), :])
            total += thrice(facey[x, pl.ds(1, own_y), :]) * (c - sol[x + 1, pl.ds(9, own_y), :])
            total += thrice(facey[x, pl.ds(0, own_y), :]) * (c - sol[x + 1, pl.ds(7, own_y), :])
            res[1, x, pl.ds(8, own_y), :] = res[0, x, pl.ds(8, own_y), :] - total
            return carry

        lax.fori_loop(0, own_x, row, 0)

    def store_copy(i):
        return pltpu.make_async_copy(outbuf.at[pl.ds(2 * i, 2)], out_hbm.at[pl.ds(2 * i, 2)], out_sem.at[i])

    def correct_last(lifted):
        def step(i, carry):
            co = dot(bcor[i], lifted)
            for j in range(2):
                value = fine[2 * i + j, pl.ds(OV, own_y), :] + co[j * own_y : (j + 1) * own_y]
                outbuf[2 * i + j] = sol[2 * i + j + 1, pl.ds(8, own_y), :] + value
            store_copy(i).start()
            return carry

        lax.fori_loop(0, own_x // 2, step, 0)

    load_rhs.wait()
    restrict(0)
    pack_y(0)
    pl.semaphore_wait(barrier, greets)
    gather_start(0)
    y_copy(0, 0).start()
    y_copy(0, 1).start()
    each_grp(lambda d: c_copy(d).start())
    c_local.start()
    for slot in range(4):
        cond_copy(slot).start()
    gather_forward(0)
    y_wait(0, 0)
    y_wait(0, 1)
    unpack_y(0)
    assemble(0)
    x_copy(0, 0).start()
    x_copy(0, 1).start()
    each_grp(lambda d: c_copy(d).wait_recv())
    c_local.wait()
    csplit[0], csplit[1] = split(cblk[...])
    load_inv.wait()
    gather_finish(0)
    coarse_multiply(0)
    each_grp(lambda d: rs_copy(0, d).start())
    fine_mid(0)
    make_faces()
    finish_x(0)
    fine_edge(0)
    correct_first(lift(0))
    for side in range(4):
        ex_copy(side).start()

    finish_sol()
    second_residual()
    restrict(1)
    gather_start(1)
    pack_y(1)
    y_copy(1, 0).start()
    y_copy(1, 1).start()
    gather_forward(1)
    y_wait(1, 0)
    y_wait(1, 1)
    unpack_y(1)
    assemble(1)
    x_copy(1, 0).start()
    x_copy(1, 1).start()
    gather_finish(1)
    coarse_multiply(1)
    each_grp(lambda d: rs_copy(1, d).start())
    fine_mid(1)
    finish_x(1)
    fine_edge(1)
    correct_last(lift(1))

    each_grp(lambda d: c_copy(d).wait_send())
    for slot in range(4):
        cond_copy(slot).wait_send()
        ex_copy(slot).wait_send()
    for it in range(2):
        each_grp(lambda d: rs_copy(it, d).wait_send())
        for d in range(1, NZ):
            z_copy(it, d).wait_send()
        for d in range(1, n_y):
            for src_d in range(NZ):
                y_forward(it, d, src_d).wait_send()
        for side in range(2):
            y_copy(it, side).wait_send()
            x_copy(it, side).wait_send()

    def stored(i, carry):
        store_copy(i).wait()
        return carry

    lax.fori_loop(0, own_x // 2, stored, 0)


def on_device(rhs, conductivity, local_inverse, coarse_basis, coarse_inverse):
    own_x, own_y, columns = rhs.shape
    modes = coarse_basis.shape[2]
    n_grp, n_mem = lax.axis_size("grp"), lax.axis_size("mem")
    n_y = n_mem // NZ
    span_x, span_y = own_x + 2 * OV, own_y + 2 * OV
    basis_t = jnp.transpose(coarse_basis, (0, 2, 1))
    anywhere = pl.BlockSpec(memory_space=pl.ANY)
    vmem = pl.BlockSpec(memory_space=pltpu.VMEM)
    dma = pltpu.SemaphoreType.DMA
    scratch = [
        pltpu.VMEM((own_x * span_y, span_x * span_y), BF16),
        pltpu.VMEM((2, own_x, own_y + 16, columns), F32),
        pltpu.VMEM((2, span_x * span_y, columns), BF16),
        pltpu.VMEM((own_x, span_y, columns), F32),
        pltpu.VMEM((own_x + 2, own_y + 16, columns), F32),
        pltpu.VMEM((own_x, own_y, columns), F32),
        pltpu.VMEM((own_x + 2, own_y + 16, 128), F32),
        pltpu.VMEM((own_x + 1, own_y, 128), F32),
        pltpu.VMEM((own_x, own_y + 8, 128), F32),
        pltpu.VMEM((own_x // 2, 2 * modes, 2 * own_y), BF16),
        pltpu.VMEM((own_x // 2, 2 * own_y, 3 * modes), BF16),
        pltpu.VMEM((2, n_mem * modes, columns), F32),
        pltpu.VMEM((n_grp * modes, n_mem * modes), F32),
        pltpu.VMEM((2, n_grp * modes, n_mem * modes), BF16),
        pltpu.VMEM((2, n_grp * modes, columns), F32),
        pltpu.VMEM((2, n_grp, modes, columns), F32),
        pltpu.VMEM((2, 2, own_x * OV, columns), BF16),
        pltpu.VMEM((2, 2, own_x * OV, columns), BF16),
        pltpu.VMEM((2, own_x, columns), F32),
        pltpu.VMEM((2, own_x, columns), F32),
        pltpu.VMEM((4, own_x, own_y), F32),
        dma((2,)), dma((own_x // 2,)), dma,
        dma((n_grp,)), dma((n_grp,)), dma((4,)), dma((4,)),
        dma((2, NZ)), dma((2, NZ)), dma((2, n_y, NZ)), dma((2, n_y, NZ)),
        dma((2, n_grp)), dma((2, n_grp)),
        dma((2, 2)), dma((2, 2)), dma((2, 2)), dma((2, 2)), dma((4,)), dma((4,)),
    ]
    return pl.pallas_call(
        functools.partial(kernel, n_grp, n_mem, own_x, own_y),
        out_shape=jax.ShapeDtypeStruct(rhs.shape, F32),
        in_specs=[anywhere, vmem, anywhere, vmem, anywhere],
        out_specs=anywhere,
        scratch_shapes=scratch,
        compiler_params=pltpu.CompilerParams(
            collective_id=0, has_side_effects=True, vmem_limit_bytes=56 * 1024 * 1024
        ),
    )(rhs, conductivity, local_inverse, basis_t, coarse_inverse)


def solution(mesh):
    placed = (
        P("grp", "mem", None),
        P("grp", "mem"),
        P(("grp", "mem"), None),
        P("grp", "mem", None),
        P(("grp", "mem"), None),
    )
    return jax.shard_map(
        on_device, mesh=mesh, in_specs=placed, out_specs=P("grp", "mem", None), check_vma=False
    )
```

```python
import functools
import jax
import jax.numpy as jnp
from jax import lax
from jax.experimental import pallas as pl
from jax.experimental.pallas import tpu as pltpu
from jax.sharding import PartitionSpec as P

OV = 4
NZ = 4
MESH = pl.DeviceIdType.MESH
F32 = jnp.float32
BF16 = jnp.bfloat16


def split(v):
    hi = v.astype(BF16)
    lo = (v - hi.astype(F32)).astype(BF16)
    return hi, lo


def dot(a, b):
    return jnp.dot(a, b, preferred_element_type=F32)


def kernel(
    n_grp, n_mem, own_x, own_y,
    rhs_hbm, cond_hbm, linv_hbm, basis_hbm, cinv_hbm,
    base_out, lifted_out, bcor_out,
    cond, basis_t, lbuf, res, win, fine, sol, cpad, facex, facey, inner_y,
    bres, bcor, bedge, rblk, cblk, csplit, part, qbuf,
    ysend, yrecv, esend, erecv, condrecv,
    in_sem, cloc_sem,
    c_send, c_recv, cond_send, cond_recv,
    az_send, az_recv, ay_send, ay_recv, rs_send, rs_recv,
    yh_send, yh_recv, xh_send, xh_recv, ex_send, ex_recv,
):
    g = lax.axis_index("grp")
    m = lax.axis_index("mem")
    n_y = n_mem // NZ
    my = m // NZ
    mz = lax.rem(m, NZ)
    span_y = own_y + 2 * OV
    columns = rhs_hbm.shape[2]
    modes = basis_hbm.shape[1]
    edge = OV * span_y
    mid = own_x * span_y
    g_up = lax.rem(g + 1, n_grp)
    g_dn = lax.rem(g + n_grp - 1, n_grp)
    m_up = lax.rem(m + 1, n_mem)
    m_dn = lax.rem(m + n_mem - 1, n_mem)

    def z_peer(d):
        return my * NZ + lax.rem(mz + d, NZ)

    def y_peer(d):
        return lax.rem(my + d, n_y) * NZ + mz

    load_rhs = pltpu.make_async_copy(rhs_hbm, res.at[0, :, pl.ds(8, own_y), :], in_sem.at[0])
    load_inv = pltpu.make_async_copy(linv_hbm.at[pl.ds(edge, mid), :], lbuf, in_sem.at[1])
    load_cond = pltpu.make_async_copy(cond_hbm, cond, in_sem.at[2])
    load_basis = pltpu.make_async_copy(basis_hbm, basis_t, in_sem.at[3])
    load_basis.start()
    load_rhs.start()
    load_cond.start()
    load_inv.start()

    barrier = pltpu.get_barrier_semaphore()

    def greet_grp(d, carry):
        pl.semaphore_signal(
            barrier, inc=1, device_id={"grp": lax.rem(g + d, n_grp)}, device_id_type=MESH
        )
        return carry

    lax.fori_loop(1, n_grp, greet_grp, 0)
    greets = n_grp - 1
    for peer in [z_peer(d) for d in range(1, NZ)] + [y_peer(d) for d in range(1, n_y)] + [m_up, m_dn]:
        pl.semaphore_signal(barrier, inc=1, device_id={"mem": peer}, device_id_type=MESH)
        greets += 1

    def wide_basis(i):
        return split(jnp.concatenate([basis_t[2 * i], basis_t[2 * i + 1]], axis=1))

    load_basis.wait()
    for i in range(own_x // 2):
        bres[i] = jnp.concatenate(wide_basis(i), axis=0)

    def prepare_basis():
        for i in range(own_x // 2):
            hi, lo = (v.astype(F32) for v in wide_basis(i))
            tall = jnp.transpose(jnp.concatenate([hi, lo, hi], axis=0))
            bcor[i] = tall.astype(BF16)
            for j in range(2):
                x = 2 * i + j
                bedge[pl.ds(x, 1), :] = tall[j * own_y : j * own_y + 1]
                bedge[pl.ds(own_x + x, 1), :] = tall[(j + 1) * own_y - 1 : (j + 1) * own_y]
        bcor_out[...] = bcor[...]

    own_rows = pl.ds(pl.multiple_of(m * modes, modes), modes)

    def restrict(it):
        def step(i, total):
            pair = res[it, pl.ds(2 * i, 2), pl.ds(8, own_y), :].reshape(2 * own_y, columns)
            hi, lo = split(pair)
            both = dot(bres[i], hi)
            return total + both[:modes] + both[modes:] + dot(bres[i, pl.ds(0, modes), :], lo)

        total = lax.fori_loop(0, own_x // 2, step, jnp.zeros((modes, columns), F32), unroll=True)
        rblk[it, own_rows, :] = total

    low_half = lax.broadcasted_iota(jnp.int32, (own_x // 2, 8, columns), 1) < OV

    def flip(v):
        return pltpu.roll(v, OV, 1)

    def pack_y(it):
        left = res[it, :, pl.ds(8, 8), :].reshape(own_x // 2, 2, 8, columns)
        right = res[it, :, pl.ds(own_y, 8), :].reshape(own_x // 2, 2, 8, columns)
        lo_side = jnp.where(low_half, left[:, 0], flip(left[:, 1]))
        hi_side = jnp.where(low_half, flip(right[:, 0]), right[:, 1])
        ysend[it, 0] = lo_side.reshape(own_x * OV, columns).astype(BF16)
        ysend[it, 1] = hi_side.reshape(own_x * OV, columns).astype(BF16)

    def y_copy(it, side):
        return pltpu.make_async_remote_copy(
            src_ref=ysend.at[it, side],
            dst_ref=yrecv.at[it, 1 - side],
            send_sem=yh_send.at[it, side],
            recv_sem=yh_recv.at[it, 1 - side],
            device_id={"mem": m_dn if side == 0 else m_up},
            device_id_type=MESH,
        )

    def y_wait(it, side):
        pltpu.make_async_remote_copy(
            src_ref=ysend.at[it, side], dst_ref=yrecv.at[it, side],
            send_sem=yh_send.at[it, side], recv_sem=yh_recv.at[it, side],
            device_id={"mem": m_dn if side == 0 else m_up}, device_id_type=MESH,
        ).wait_recv()

    def unpack_y(it):
        low = jnp.where(m == 0, 0.0, yrecv[it, 0].astype(F32)).reshape(own_x // 2, 8, columns)
        high = jnp.where(m == n_mem - 1, 0.0, yrecv[it, 1].astype(F32)).reshape(own_x // 2, 8, columns)
        low_even, high_odd = flip(low), flip(high)
        for i in range(own_x // 2):
            res[it, 2 * i, pl.ds(0, 8), :] = low_even[i]
            res[it, 2 * i + 1, pl.ds(0, 8), :] = low[i]
            res[it, 2 * i, pl.ds(own_y + 8, 8), :] = high[i]
            res[it, 2 * i + 1, pl.ds(own_y + 8, 8), :] = high_odd[i]

    def assemble(it):
        def row(x, carry):
            start = pl.multiple_of((x + OV) * span_y, span_y)
            win[it, pl.ds(start, span_y), :] = res[it, x, pl.ds(8 - OV, span_y), :].astype(BF16)
            return carry

        lax.fori_loop(0, own_x, row, 0)

    def x_copy(it, side):
        src = edge if side == 0 else mid
        dst = edge + mid if side == 0 else 0
        return pltpu.make_async_remote_copy(
            src_ref=win.at[it, pl.ds(src, edge), :],
            dst_ref=win.at[it, pl.ds(dst, edge), :],
            send_sem=xh_send.at[it, side],
            recv_sem=xh_recv.at[it, 1 - side],
            device_id={"grp": g_dn if side == 0 else g_up},
            device_id_type=MESH,
        )

    def x_wait(it, side):
        dst = 0 if side == 0 else edge + mid
        pltpu.make_async_remote_copy(
            src_ref=win.at[it, pl.ds(dst, edge), :],
            dst_ref=win.at[it, pl.ds(dst, edge), :],
            send_sem=xh_send.at[it, side],
            recv_sem=xh_recv.at[it, side],
            device_id={"grp": g_dn if side == 0 else g_up},
            device_id_type=MESH,
        ).wait_recv()

    def finish_x(it):
        x_wait(it, 0)
        x_wait(it, 1)

        @pl.when(g == 0)
        def _():
            win[it, pl.ds(0, edge), :] = jnp.zeros((edge, columns), BF16)

        @pl.when(g == n_grp - 1)
        def _():
            win[it, pl.ds(edge + mid, edge), :] = jnp.zeros((edge, columns), BF16)

    chunk = OV * span_y

    def fine_mid(it):
        def step(i, carry):
            rows = pl.ds(pl.multiple_of(i * chunk, chunk), chunk)
            got = dot(lbuf[rows, pl.ds(edge, mid)], win[it, pl.ds(edge, mid), :])
            fine[pl.ds(i * OV, OV)] = got.reshape(OV, span_y, columns)
            return carry

        lax.fori_loop(0, own_x // OV, step, 0)

    def fine_edge(it):
        def step(i, carry):
            rows = pl.ds(pl.multiple_of(i * chunk, chunk), chunk)
            got = dot(lbuf[rows, pl.ds(0, edge)], win[it, pl.ds(0, edge), :])
            got += dot(lbuf[rows, pl.ds(edge + mid, edge)], win[it, pl.ds(edge + mid, edge), :])
            fine[pl.ds(i * OV, OV)] += got.reshape(OV, span_y, columns)
            return carry

        lax.fori_loop(0, own_x // OV, step, 0)

    def z_copy(it, d):
        return pltpu.make_async_remote_copy(
            src_ref=rblk.at[it, own_rows, :], dst_ref=rblk.at[it, own_rows, :],
            send_sem=az_send.at[it, d], recv_sem=az_recv.at[it, d],
            device_id={"mem": z_peer(d)}, device_id_type=MESH,
        )

    def y_forward(it, d, src_d):
        block = my * NZ + lax.rem(mz + NZ - src_d, NZ)
        rows = pl.ds(pl.multiple_of(block * modes, modes), modes)
        return pltpu.make_async_remote_copy(
            src_ref=rblk.at[it, rows, :], dst_ref=rblk.at[it, rows, :],
            send_sem=ay_send.at[it, d, src_d], recv_sem=ay_recv.at[it, d, src_d],
            device_id={"mem": y_peer(d)}, device_id_type=MESH,
        )

    def gather_start(it):
        for d in range(1, NZ):
            z_copy(it, d).start()
        for d in range(1, n_y):
            y_forward(it, d, 0).start()

    def gather_forward(it):
        for src_d in (1, 3, 2):
            z_copy(it, src_d).wait_recv()
            for d in range(1, n_y):
                y_forward(it, d, src_d).start()

    def gather_finish(it):
        for src_d in range(NZ):
            for d in range(1, n_y):
                y_forward(it, d, src_d).wait_recv()

    def c_copy(d):
        dest = lax.rem(g + d, n_grp)
        return pltpu.make_async_remote_copy(
            src_ref=cinv_hbm.at[:, pl.ds(pl.multiple_of(dest * n_mem * modes, n_mem * modes), n_mem * modes)],
            dst_ref=cblk.at[pl.ds(pl.multiple_of(g * modes, modes), modes), :],
            send_sem=c_send.at[d], recv_sem=c_recv.at[d],
            device_id={"grp": dest}, device_id_type=MESH,
        )

    c_local = pltpu.make_async_copy(
        cinv_hbm.at[:, pl.ds(pl.multiple_of(g * n_mem * modes, n_mem * modes), n_mem * modes)],
        cblk.at[pl.ds(pl.multiple_of(g * modes, modes), modes), :],
        cloc_sem,
    )

    def each_grp(action):
        def body(d, carry):
            action(d)
            return carry

        lax.fori_loop(1, n_grp, body, 0)

    def coarse_multiply(it):
        hi, lo = split(rblk[it])

        def step(i, carry):
            rows = pl.ds(pl.multiple_of(i * 64, 64), 64)
            c_hi, c_lo = csplit[0, rows, :], csplit[1, rows, :]
            part[it, rows, :] = dot(c_hi, hi) + (dot(c_hi, lo) + dot(c_lo, hi))
            return carry

        lax.fori_loop(0, n_grp * modes // 64, step, 0)

    def rs_copy(it, d):
        dest = lax.rem(g + d, n_grp)
        return pltpu.make_async_remote_copy(
            src_ref=part.at[it, pl.ds(pl.multiple_of(dest * modes, modes), modes), :],
            dst_ref=qbuf.at[it, d],
            send_sem=rs_send.at[it, d], recv_sem=rs_recv.at[it, d],
            device_id={"grp": dest}, device_id_type=MESH,
        )

    def lift(it):
        each_grp(lambda d: rs_copy(it, d).wait_recv())

        def add(d, total):
            return total + qbuf[it, d]

        own = part[it, pl.ds(pl.multiple_of(g * modes, modes), modes), :]
        lifted = lax.fori_loop(1, n_grp, add, own)
        hi, lo = split(lifted)
        return jnp.concatenate([hi.astype(F32), hi.astype(F32), lo.astype(F32)], axis=0).astype(BF16)

    def cond_copy(slot):
        if slot < 2:
            device = {"grp": g_up if slot == 0 else g_dn}
        else:
            device = {"mem": m_up if slot == 2 else m_dn}
        return pltpu.make_async_remote_copy(
            src_ref=cond, dst_ref=condrecv.at[slot],
            send_sem=cond_send.at[slot], recv_sem=cond_recv.at[slot],
            device_id=device, device_id_type=MESH,
        )

    def cond_start():
        for slot in range(4):
            cond_copy(slot).start()

    def make_faces():
        for slot in range(4):
            cond_copy(slot).wait_recv()
        shape = (own_y, own_y)
        eye = lax.broadcasted_iota(jnp.int32, shape, 0) == lax.broadcasted_iota(jnp.int32, shape, 1)
        lane = lax.broadcasted_iota(jnp.int32, (1, own_y), 1)

        def spread(row):
            full = jnp.where(eye, jnp.broadcast_to(row, shape), 0.0)
            return jnp.broadcast_to(jnp.sum(full, axis=1, keepdims=True), (own_y, 128))

        def pick(row, at):
            one = jnp.sum(jnp.where(lane == at, row, 0.0), axis=1, keepdims=True)
            return jnp.broadcast_to(one, (8, 128))

        def row_of(x, carry):
            cpad[x + 1, pl.ds(8, own_y), :] = spread(cond[pl.ds(x, 1), :])
            low = jnp.where(m == 0, 0.0, pick(condrecv[2, pl.ds(x, 1), :], own_y - 1))
            high = jnp.where(m == n_mem - 1, 0.0, pick(condrecv[3, pl.ds(x, 1), :], 0))
            cpad[x + 1, pl.ds(0, 8), :] = low
            cpad[x + 1, pl.ds(own_y + 8, 8), :] = high
            return carry

        lax.fori_loop(0, own_x, row_of, 0, unroll=4)
        first = jnp.where(g == 0, 0.0, condrecv[0, pl.ds(own_x - 1, 1), :])
        last = jnp.where(g == n_grp - 1, 0.0, condrecv[1, pl.ds(0, 1), :])
        cpad[0, pl.ds(8, own_y), :] = spread(first)
        cpad[own_x + 1, pl.ds(8, own_y), :] = spread(last)

        at_y = lax.broadcasted_iota(jnp.int32, (own_y + 8, 128), 0)
        inside = (at_y > 0) & (at_y < own_y)

        def face_x(x, carry):
            facex[x] = 0.5 * (cpad[x, pl.ds(8, own_y), :] + cpad[x + 1, pl.ds(8, own_y), :])
            return carry

        def face_y(x, carry):
            face = 0.5 * (cpad[x + 1, pl.ds(7, own_y + 8), :] + cpad[x + 1, pl.ds(8, own_y + 8), :])
            facey[x] = face
            inner_y[x] = jnp.where(inside, face, 0.0)
            return carry

        lax.fori_loop(0, own_x + 1, face_x, 0)
        lax.fori_loop(0, own_x, face_y, 0)

    def ex_copy(side):
        if side < 2:
            src = sol.at[1 if side == 0 else own_x, pl.ds(8, own_y), :]
            dst = sol.at[own_x + 1 if side == 0 else 0, pl.ds(8, own_y), :]
            device = {"grp": g_dn if side == 0 else g_up}
        else:
            src = esend.at[side - 2]
            dst = erecv.at[side - 2]
            device = {"mem": m_dn if side == 2 else m_up}
        return pltpu.make_async_remote_copy(
            src_ref=src, dst_ref=dst, send_sem=ex_send.at[side], recv_sem=ex_recv.at[side],
            device_id=device, device_id_type=MESH,
        )

    def sol_rows(i, lifted):
        co = dot(bcor[i], lifted)
        for j in range(2):
            value = fine[2 * i + j, pl.ds(OV, own_y), :] + co[j * own_y : (j + 1) * own_y]
            sol[2 * i + j + 1, pl.ds(8, own_y), :] = value

    def correct_edges(lifted):
        co = dot(bedge[...].astype(BF16), lifted)
        esend[0] = fine[:, OV, :] + co[:own_x]
        esend[1] = fine[:, OV + own_y - 1, :] + co[own_x:]
        sol_rows(0, lifted)
        sol_rows(own_x // 2 - 1, lifted)

    def ex_start():
        for side in range(4):
            ex_copy(side).start()

    def correct_inner(lifted):
        def step(i, carry):
            sol_rows(i, lifted)
            return carry

        lax.fori_loop(1, own_x // 2 - 1, step, 0, unroll=True)

    def zero_margin():
        zero = jnp.zeros((8, columns), F32)
        for x in range(own_x):
            sol[x + 1, pl.ds(0, 8), :] = zero
            sol[x + 1, pl.ds(own_y + 8, 8), :] = zero

    def thrice(v):
        return jnp.concatenate([v] * (columns // 128), axis=1)

    def inner_residual():
        def row(x, first, last):
            c = sol[x + 1, pl.ds(8, own_y), :]
            total = thrice(inner_y[x, pl.ds(1, own_y), :]) * (c - sol[x + 1, pl.ds(9, own_y), :])
            total += thrice(inner_y[x, pl.ds(0, own_y), :]) * (c - sol[x + 1, pl.ds(7, own_y), :])
            if not last:
                total += thrice(facex[x + 1]) * (c - sol[x + 2, pl.ds(8, own_y), :])
            if not first:
                total += thrice(facex[x]) * (c - sol[x, pl.ds(8, own_y), :])
            res[1, x, pl.ds(8, own_y), :] = res[0, x, pl.ds(8, own_y), :] - total

        def step(x, carry):
            row(x, False, False)
            return carry

        row(0, True, False)
        lax.fori_loop(1, own_x - 1, step, 0, unroll=2)
        row(own_x - 1, False, True)

    def outer_residual():
        for side in range(4):
            ex_copy(side).wait_recv()
        low_x = jnp.where(g == 0, 0.0, sol[0, pl.ds(8, own_y), :])
        high_x = jnp.where(g == n_grp - 1, 0.0, sol[own_x + 1, pl.ds(8, own_y), :])
        res[1, 0, pl.ds(8, own_y), :] -= thrice(facex[0]) * (sol[1, pl.ds(8, own_y), :] - low_x)
        res[1, own_x - 1, pl.ds(8, own_y), :] -= thrice(facex[own_x]) * (
            sol[own_x, pl.ds(8, own_y), :] - high_x
        )
        low_y = thrice(facey[:, 0, :]) * (esend[0] - jnp.where(m == 0, 0.0, erecv[1]))
        high_y = thrice(facey[:, own_y, :]) * (esend[1] - jnp.where(m == n_mem - 1, 0.0, erecv[0]))
        res[1, :, 8, :] -= low_y
        res[1, :, own_y + 7, :] -= high_y

    def finish_base():
        def step(x, carry):
            base_out[x] = sol[x + 1, pl.ds(8, own_y), :] + fine[x, pl.ds(OV, own_y), :]
            return carry

        lax.fori_loop(0, own_x, step, 0, unroll=2)

    load_rhs.wait()
    restrict(0)
    pl.semaphore_wait(barrier, greets)
    gather_start(0)
    pack_y(0)
    y_copy(0, 0).start()
    y_copy(0, 1).start()
    load_cond.wait()
    cond_start()
    each_grp(lambda d: c_copy(d).start())
    c_local.start()
    prepare_basis()
    zero_margin()
    gather_forward(0)
    make_faces()
    y_wait(0, 0)
    y_wait(0, 1)
    unpack_y(0)
    assemble(0)
    x_copy(0, 0).start()
    x_copy(0, 1).start()
    gather_finish(0)
    each_grp(lambda d: c_copy(d).wait_recv())
    c_local.wait()
    csplit[0], csplit[1] = split(cblk[...])
    coarse_multiply(0)
    each_grp(lambda d: rs_copy(0, d).start())
    load_inv.wait()
    fine_mid(0)
    finish_x(0)
    fine_edge(0)
    lifted = lift(0)
    correct_edges(lifted)
    ex_start()
    correct_inner(lifted)
    inner_residual()

    outer_residual()
    restrict(1)
    gather_start(1)
    pack_y(1)
    gather_forward(1)
    y_copy(1, 0).start()
    y_copy(1, 1).start()
    y_wait(1, 0)
    y_wait(1, 1)
    unpack_y(1)
    assemble(1)
    x_copy(1, 0).start()
    x_copy(1, 1).start()
    gather_finish(1)
    coarse_multiply(1)
    each_grp(lambda d: rs_copy(1, d).start())
    fine_mid(1)
    finish_x(1)
    fine_edge(1)
    finish_base()
    lifted_out[...] = lift(1)

    each_grp(lambda d: c_copy(d).wait_send())
    for slot in range(4):
        cond_copy(slot).wait_send()
        ex_copy(slot).wait_send()
    for it in range(2):
        each_grp(lambda d: rs_copy(it, d).wait_send())
        for d in range(1, NZ):
            z_copy(it, d).wait_send()
        for d in range(1, n_y):
            for src_d in range(NZ):
                y_forward(it, d, src_d).wait_send()
        for side in range(2):
            y_copy(it, side).wait_send()
            x_copy(it, side).wait_send()


def tail_kernel(base, lifted, bcor, out_hbm, outbuf, out_sem):
    pairs, own_y = base.shape[0] // 2, base.shape[1]
    per = 3

    def store(i):
        rows = pl.ds(2 * per * i, 2 * per)
        return pltpu.make_async_copy(outbuf.at[rows], out_hbm.at[rows], out_sem.at[i])

    for i in range(pairs // per):
        for k in range(per * i, per * i + per):
            co = dot(bcor[k], lifted[...])
            for j in range(2):
                outbuf[2 * k + j] = base[2 * k + j] + co[j * own_y : (j + 1) * own_y]
        store(i).start()
    for i in range(pairs // per):
        store(i).wait()


def on_device(rhs, conductivity, local_inverse, coarse_basis, coarse_inverse):
    own_x, own_y, columns = rhs.shape
    modes = coarse_basis.shape[2]
    n_grp, n_mem = lax.axis_size("grp"), lax.axis_size("mem")
    n_y = n_mem // NZ
    span_x, span_y = own_x + 2 * OV, own_y + 2 * OV
    basis_t = jnp.transpose(coarse_basis, (0, 2, 1))
    arrays = (rhs, conductivity, local_inverse, basis_t, coarse_inverse)
    hbm = pl.BlockSpec(memory_space=pltpu.HBM)
    vmem = pl.BlockSpec(memory_space=pltpu.VMEM)
    dma = pltpu.SemaphoreType.DMA
    scratch = [
        pltpu.VMEM((own_x, own_y), F32),
        pltpu.VMEM((own_x, modes, own_y), F32),
        pltpu.VMEM((own_x * span_y, span_x * span_y), BF16),
        pltpu.VMEM((2, own_x, own_y + 16, columns), F32),
        pltpu.VMEM((2, span_x * span_y, columns), BF16),
        pltpu.VMEM((own_x, span_y, columns), F32),
        pltpu.VMEM((own_x + 2, own_y + 16, columns), F32),
        pltpu.VMEM((own_x + 2, own_y + 16, 128), F32),
        pltpu.VMEM((own_x + 1, own_y, 128), F32),
        pltpu.VMEM((own_x, own_y + 8, 128), F32),
        pltpu.VMEM((own_x, own_y + 8, 128), F32),
        pltpu.VMEM((own_x // 2, 2 * modes, 2 * own_y), BF16),
        pltpu.VMEM((own_x // 2, 2 * own_y, 3 * modes), BF16),
        pltpu.VMEM((2 * own_x, 3 * modes), F32),
        pltpu.VMEM((2, n_mem * modes, columns), F32),
        pltpu.VMEM((n_grp * modes, n_mem * modes), F32),
        pltpu.VMEM((2, n_grp * modes, n_mem * modes), BF16),
        pltpu.VMEM((2, n_grp * modes, columns), F32),
        pltpu.VMEM((2, n_grp, modes, columns), F32),
        pltpu.VMEM((2, 2, own_x * OV, columns), BF16),
        pltpu.VMEM((2, 2, own_x * OV, columns), BF16),
        pltpu.VMEM((2, own_x, columns), F32),
        pltpu.VMEM((2, own_x, columns), F32),
        pltpu.VMEM((4, own_x, own_y), F32),
        dma((4,)), dma,
        dma((n_grp,)), dma((n_grp,)), dma((4,)), dma((4,)),
        dma((2, NZ)), dma((2, NZ)), dma((2, n_y, NZ)), dma((2, n_y, NZ)),
        dma((2, n_grp)), dma((2, n_grp)),
        dma((2, 2)), dma((2, 2)), dma((2, 2)), dma((2, 2)), dma((4,)), dma((4,)),
    ]
    base, lifted, bcor = pl.pallas_call(
        functools.partial(kernel, n_grp, n_mem, own_x, own_y),
        out_shape=(
            jax.ShapeDtypeStruct(rhs.shape, F32),
            jax.ShapeDtypeStruct((3 * modes, columns), BF16),
            jax.ShapeDtypeStruct((own_x // 2, 2 * own_y, 3 * modes), BF16),
        ),
        in_specs=[hbm] * 5,
        out_specs=(vmem, vmem, vmem),
        scratch_shapes=scratch,
        compiler_params=pltpu.CompilerParams(
            collective_id=0, has_side_effects=True, vmem_limit_bytes=44 * 1024 * 1024
        ),
    )(*(pltpu.with_memory_space_constraint(v, pltpu.HBM) for v in arrays))
    return pl.pallas_call(
        tail_kernel,
        out_shape=jax.ShapeDtypeStruct(rhs.shape, F32),
        in_specs=[vmem, vmem, vmem],
        out_specs=hbm,
        scratch_shapes=[pltpu.VMEM(rhs.shape, F32), dma((own_x // 6,))],
        compiler_params=pltpu.CompilerParams(vmem_limit_bytes=16 * 1024 * 1024),
    )(base, lifted, bcor)


def solution(mesh):
    placed = (
        P("grp", "mem", None),
        P("grp", "mem"),
        P(("grp", "mem"), None),
        P("grp", "mem", None),
        P(("grp", "mem"), None),
    )
    return jax.shard_map(
        on_device, mesh=mesh, in_specs=placed, out_specs=P("grp", "mem", None), check_vma=False
    )
```

```python
import functools
import jax
import jax.numpy as jnp
from jax import lax
from jax.experimental import pallas as pl
from jax.experimental.pallas import tpu as pltpu
from jax.sharding import PartitionSpec as P

OV = 4
LANES = 128
NZ = 4
MESH = pl.DeviceIdType.MESH
F32 = jnp.float32
BF16 = jnp.bfloat16


def split(v):
    hi = v.astype(BF16)
    lo = (v - hi.astype(F32)).astype(BF16)
    return hi, lo


def dot(a, b):
    return jnp.dot(a, b, preferred_element_type=F32)


def kernel(
    n_grp, n_mem, own_x, own_y,
    rhs_hbm, cond_hbm, linv_hbm, basis_hbm, cinv_hbm,
    base_out, lifted_out, bcor_out,
    cond, basis_t, lbuf, res, win, wmar, lmar, ysel, fine, sol, cpad, facex, facey, inner_y,
    bres, bcor, bedge, rblk, cblk, csplit, part, pairbuf, sumbuf, qbuf,
    ysend, xsend, esend, erecv, condrecv,
    in_sem, cloc_sem,
    c_send, c_recv, cond_send, cond_recv,
    az_send, az_recv, ay_send, ay_recv, pr_send, pr_recv, rs_send, rs_recv,
    yh_send, yh_recv, xh_send, xh_recv, co_send, co_recv, ex_send, ex_recv,
):
    g = lax.axis_index("grp")
    m = lax.axis_index("mem")
    n_y = n_mem // NZ
    my = m // NZ
    mz = lax.rem(m, NZ)
    n_pair = n_grp // 2
    pair = g // 2
    core = lax.rem(g, 2)
    span_y = own_y + 2 * OV
    columns = rhs_hbm.shape[2]
    modes = basis_hbm.shape[1]
    chunks = columns // LANES
    edge = OV * span_y
    y_margin = own_x * OV

    def y_rows(side):
        return pl.ds(2 * edge + side * y_margin, y_margin)

    def x_rows(side):
        return pl.ds(side * edge, OV * own_y)

    mid = own_x * span_y
    g_up = lax.rem(g + 1, n_grp)
    g_dn = lax.rem(g + n_grp - 1, n_grp)
    m_up = lax.rem(m + 1, n_mem)
    m_dn = lax.rem(m + n_mem - 1, n_mem)

    def z_peer(d):
        return my * NZ + lax.rem(mz + d, NZ)

    def y_peer(d):
        return lax.rem(my + d, n_y) * NZ + mz

    def wait_bytes(ref, sem):
        pltpu.make_async_copy(ref, ref, sem).wait()

    load_rhs = pltpu.make_async_copy(rhs_hbm, res.at[0, :, pl.ds(8, own_y), :], in_sem.at[0])
    load_inv = pltpu.make_async_copy(linv_hbm.at[pl.ds(edge, mid), :], lbuf, in_sem.at[1])
    load_cond = pltpu.make_async_copy(cond_hbm, cond, in_sem.at[2])
    load_basis = pltpu.make_async_copy(basis_hbm, basis_t, in_sem.at[3])
    load_basis.start()
    load_rhs.start()
    load_cond.start()
    load_inv.start()

    barrier = pltpu.get_barrier_semaphore()

    def greet_grp(d, carry):
        pl.semaphore_signal(
            barrier, inc=1, device_id={"grp": lax.rem(g + d, n_grp)}, device_id_type=MESH
        )
        return carry

    lax.fori_loop(1, n_grp, greet_grp, 0)
    greets = n_grp - 1
    for peer in [z_peer(d) for d in range(1, NZ)] + [y_peer(d) for d in range(1, n_y)] + [m_up, m_dn]:
        pl.semaphore_signal(barrier, inc=1, device_id={"mem": peer}, device_id_type=MESH)
        greets += 1
    for g_side in (g_dn, g_up):
        for m_side in (m_dn, m_up):
            pl.semaphore_signal(
                barrier, inc=1, device_id={"grp": g_side, "mem": m_side}, device_id_type=MESH
            )
            greets += 1

    def wide_basis(i):
        return split(jnp.concatenate([basis_t[2 * i], basis_t[2 * i + 1]], axis=1))

    load_basis.wait()
    for i in range(own_x // 2):
        bres[i] = jnp.concatenate(wide_basis(i), axis=0)

    def prepare_basis():
        for i in range(own_x // 2):
            hi, lo = (v.astype(F32) for v in wide_basis(i))
            tall = jnp.transpose(jnp.concatenate([hi, lo, hi], axis=0))
            bcor[i] = tall.astype(BF16)
            for j in range(2):
                x = 2 * i + j
                bedge[pl.ds(x, 1), :] = tall[j * own_y : j * own_y + 1]
                bedge[pl.ds(own_x + x, 1), :] = tall[(j + 1) * own_y - 1 : (j + 1) * own_y]
        bcor_out[...] = bcor[...]

    own_rows = pl.ds(pl.multiple_of(m * modes, modes), modes)

    def restrict(it):
        def step(i, total):
            pair = res[it, pl.ds(2 * i, 2), pl.ds(8, own_y), :].reshape(2 * own_y, columns)
            hi, lo = split(pair)
            both = dot(bres[i], hi)
            return total + both[:modes] + both[modes:] + dot(bres[i, pl.ds(0, modes), :], lo)

        total = lax.fori_loop(0, own_x // 2, step, jnp.zeros((modes, columns), F32), unroll=True)
        for c in range(chunks):
            rblk[it, c, own_rows, :] = total[:, c * LANES : (c + 1) * LANES]

    low_half = lax.broadcasted_iota(jnp.int32, (own_x // 2, 8, columns), 1) < OV

    def flip(v):
        return pltpu.roll(v, OV, 1)

    def pack_y(it):
        left = res[it, :, pl.ds(8, 8), :].reshape(own_x // 2, 2, 8, columns)
        right = res[it, :, pl.ds(own_y, 8), :].reshape(own_x // 2, 2, 8, columns)
        lo_side = jnp.where(low_half, left[:, 0], flip(left[:, 1]))
        hi_side = jnp.where(low_half, flip(right[:, 0]), right[:, 1])
        ysend[it, 0] = lo_side.reshape(own_x * OV, columns).astype(BF16)
        ysend[it, 1] = hi_side.reshape(own_x * OV, columns).astype(BF16)

    def y_copy(it, side):
        return pltpu.make_async_remote_copy(
            src_ref=ysend.at[it, side],
            dst_ref=wmar.at[it, y_rows(1 - side), :],
            send_sem=yh_send.at[it, side],
            recv_sem=yh_recv.at[it, 1 - side],
            device_id={"mem": m_dn if side == 0 else m_up},
            device_id_type=MESH,
        )

    def finish_y(it):
        y_copy(it, 1).wait_recv()
        y_copy(it, 0).wait_recv()
        for side, last in ((0, 0), (1, n_mem - 1)):

            @pl.when(m == last)
            def _(side=side):
                wmar[it, y_rows(side), :] = jnp.zeros((y_margin, columns), BF16)

    def assemble(it):
        def row(x, carry):
            win[pl.ds(pl.multiple_of(x * span_y, span_y), span_y), :] = res[
                it, x, pl.ds(8 - OV, span_y), :
            ].astype(BF16)
            return carry

        lax.fori_loop(0, own_x, row, 0, unroll=4)

    def pack_x(it):
        for side, first in ((0, 0), (1, own_x - OV)):
            rows = res[it, pl.ds(first, OV), pl.ds(8, own_y), :]
            xsend[it, side] = rows.reshape(OV * own_y, columns).astype(BF16)

    def x_copy(it, side):
        return pltpu.make_async_remote_copy(
            src_ref=xsend.at[it, side],
            dst_ref=wmar.at[it, x_rows(1 - side), :],
            send_sem=xh_send.at[it, side],
            recv_sem=xh_recv.at[it, 1 - side],
            device_id={"grp": g_dn if side == 0 else g_up},
            device_id_type=MESH,
        )

    def corner_copy(it, side, y_side):
        first = 0 if side == 0 else (own_x - OV) * OV
        lands = (1 - side) * edge + OV * own_y + (1 - y_side) * OV * OV
        return pltpu.make_async_remote_copy(
            src_ref=ysend.at[it, y_side, pl.ds(first, OV * OV), :],
            dst_ref=wmar.at[it, pl.ds(lands, OV * OV), :],
            send_sem=co_send.at[it, side, y_side],
            recv_sem=co_recv.at[it, 1 - side, 1 - y_side],
            device_id={
                "grp": g_dn if side == 0 else g_up,
                "mem": m_dn if y_side == 0 else m_up,
            },
            device_id_type=MESH,
        )

    def corner_start(it):
        for side in range(2):
            for y_side in range(2):
                corner_copy(it, side, y_side).start()

    def finish_x(it):
        for side in range(2):
            x_copy(it, 1 - side).wait_recv()
            for y_side in range(2):
                corner_copy(it, 1 - side, 1 - y_side).wait_recv()
        for side, last in ((0, 0), (1, n_grp - 1)):

            @pl.when(g == last)
            def _(side=side):
                wmar[it, pl.ds(side * edge, edge), :] = jnp.zeros((edge, columns), BF16)

        for y_side, last in ((0, 0), (1, n_mem - 1)):

            @pl.when(m == last)
            def _(y_side=y_side):
                for side in range(2):
                    lands = side * edge + OV * own_y + y_side * OV * OV
                    wmar[it, pl.ds(lands, OV * OV), :] = jnp.zeros((OV * OV, columns), BF16)

    chunk = OV * span_y

    def selector(shape, column_of):
        out = lax.broadcasted_iota(jnp.int32, shape, 1)
        into = lax.broadcasted_iota(jnp.int32, shape, 0)
        return jnp.where(into == column_of(out), 1.0, 0.0).astype(BF16)

    def x_column(n):
        row = sum((n >= own_y * k).astype(jnp.int32) for k in range(1, OV))
        corner = n - OV * own_y
        far = (corner >= OV * OV).astype(jnp.int32)
        corner = corner - far * OV * OV
        inside = row * (span_y - own_y) + n + OV
        outside = (corner // OV) * span_y + corner % OV + far * (span_y - OV)
        return jnp.where(n < OV * own_y, inside, outside)

    def y_column(n):
        far = (n >= y_margin).astype(jnp.int32)
        n = n - far * y_margin
        return (n // OV) * span_y + n % OV + far * (span_y - OV)

    def select_x():
        pick = selector((edge, edge), x_column)

        def step(i, carry):
            rows = pl.ds(pl.multiple_of(i * chunk, chunk), chunk)
            for side, first in ((0, 0), (1, edge + mid)):
                got = dot(lbuf[rows, pl.ds(first, edge)], pick)
                lmar[rows, pl.ds(side * edge, edge)] = got.astype(BF16)
            return carry

        lax.fori_loop(0, mid // chunk, step, 0)

    def select_y(first, last):
        if first == 0:
            ysel[...] = selector((mid, 2 * y_margin), y_column)

        def step(i, carry):
            rows = pl.ds(pl.multiple_of(i * chunk, chunk), chunk)
            got = dot(lbuf[rows, pl.ds(edge, mid)], ysel[...])
            lmar[rows, pl.ds(2 * edge, 2 * y_margin)] = got.astype(BF16)
            return carry

        lax.fori_loop(first, last, step, 0)

    def fine_inner(first, last):
        def step(i, carry):
            rows = pl.ds(pl.multiple_of(i * chunk, chunk), chunk)
            got = dot(lbuf[rows, pl.ds(edge, mid)], win[...])
            fine[pl.ds(i * OV, OV)] = got.reshape(OV, span_y, columns)
            return carry

        lax.fori_loop(first, last, step, 0)

    def fine_outer(it):
        def step(i, carry):
            rows = pl.ds(pl.multiple_of(i * chunk, chunk), chunk)
            got = dot(lmar[rows, :], wmar[it])
            fine[pl.ds(i * OV, OV)] += got.reshape(OV, span_y, columns)
            return carry

        lax.fori_loop(0, own_x // OV, step, 0)

    def z_copy(it, c, d):
        return pltpu.make_async_remote_copy(
            src_ref=rblk.at[it, c, own_rows, :], dst_ref=rblk.at[it, c, own_rows, :],
            send_sem=az_send.at[it], recv_sem=az_recv.at[it, c, d],
            device_id={"mem": z_peer(d)}, device_id_type=MESH,
        )

    def y_forward(it, c, d, src_d):
        block = my * NZ + lax.rem(mz + NZ - src_d, NZ)
        rows = pl.ds(pl.multiple_of(block * modes, modes), modes)
        return pltpu.make_async_remote_copy(
            src_ref=rblk.at[it, c, rows, :], dst_ref=rblk.at[it, c, rows, :],
            send_sem=ay_send.at[it], recv_sem=ay_recv.at[it, c],
            device_id={"mem": y_peer(d)}, device_id_type=MESH,
        )

    def gather_start(it):
        for c in range(chunks):
            for d in (2, 1, 3):
                z_copy(it, c, d).start()
            for d in range(1, n_y):
                y_forward(it, c, d, 0).start()

    def gather_forward(it, c, sources):
        for src_d in sources:
            z_copy(it, c, src_d).wait_recv()
            for d in range(1, n_y):
                y_forward(it, c, d, src_d).start()

    def gather_finish(it, c):
        wait_bytes(rblk.at[it, c, pl.ds(0, (n_y - 1) * NZ * modes), :], ay_recv.at[it, c])

    def c_copy(d):
        dest = lax.rem(g + d, n_grp)
        return pltpu.make_async_remote_copy(
            src_ref=cinv_hbm.at[:, pl.ds(pl.multiple_of(dest * n_mem * modes, n_mem * modes), n_mem * modes)],
            dst_ref=cblk.at[pl.ds(pl.multiple_of(g * modes, modes), modes), :],
            send_sem=c_send, recv_sem=c_recv,
            device_id={"grp": dest}, device_id_type=MESH,
        )

    c_local = pltpu.make_async_copy(
        cinv_hbm.at[:, pl.ds(pl.multiple_of(g * n_mem * modes, n_mem * modes), n_mem * modes)],
        cblk.at[pl.ds(pl.multiple_of(g * modes, modes), modes), :],
        cloc_sem,
    )

    def each_grp(action):
        def body(d, carry):
            action(d)
            return carry

        lax.fori_loop(1, n_grp, body, 0)

    def coarse_multiply(it, c):
        hi, lo = split(rblk[it, c])
        both = jnp.concatenate([hi, lo], axis=1)

        def step(i, carry):
            rows = pl.ds(pl.multiple_of(i * 128, 128), 128)
            two = dot(csplit[0, rows, :], both)
            got = two[:, :LANES] + (two[:, LANES:] + dot(csplit[1, rows, :], hi))
            part[it, c, pl.ds(i * 4, 4)] = got.reshape(4, 2, modes, LANES)
            return carry

        lax.fori_loop(0, n_grp * modes // 128, step, 0, unroll=True)

    def pair_copy(it, c):
        return pltpu.make_async_remote_copy(
            src_ref=part.at[it, c, :, 1 - core], dst_ref=pairbuf.at[it, c],
            send_sem=pr_send.at[it, c], recv_sem=pr_recv.at[it, c],
            device_id={"grp": 2 * pair + 1 - core}, device_id_type=MESH,
        )

    def rs_copy(it, c, d):
        dest = lax.rem(pair + d, n_pair)
        return pltpu.make_async_remote_copy(
            src_ref=sumbuf.at[it, c, dest], dst_ref=qbuf.at[it, c, d],
            send_sem=rs_send.at[it], recv_sem=rs_recv.at[it, c],
            device_id={"grp": 2 * dest + core}, device_id_type=MESH,
        )

    def pair_step(it, c):
        pair_copy(it, c).wait_recv()
        sumbuf[it, c] = part[it, c, :, core] + pairbuf[it, c]
        for d in range(1, n_pair):
            rs_copy(it, c, d).start()

    def lift(it):
        pieces = []
        for c in range(chunks):
            wait_bytes(qbuf.at[it, c, pl.ds(1, n_pair - 1)], rs_recv.at[it, c])
            total = sumbuf[it, c, pair]
            for d in range(1, n_pair):
                total = total + qbuf[it, c, d]
            pieces.append(total)
        hi, lo = split(jnp.concatenate(pieces, axis=1))
        return jnp.concatenate([hi.astype(F32), hi.astype(F32), lo.astype(F32)], axis=0).astype(BF16)

    def coarse_step(it, c):
        gather_finish(it, c)
        coarse_multiply(it, c)
        pair_copy(it, c).start()

    def y_start(it):
        y_copy(it, 0).start()
        y_copy(it, 1).start()

    def x_start(it):
        x_copy(it, 0).start()
        x_copy(it, 1).start()

    def cond_copy(slot):
        if slot < 2:
            device = {"grp": g_up if slot == 0 else g_dn}
        else:
            device = {"mem": m_up if slot == 2 else m_dn}
        return pltpu.make_async_remote_copy(
            src_ref=cond, dst_ref=condrecv.at[slot],
            send_sem=cond_send, recv_sem=cond_recv,
            device_id=device, device_id_type=MESH,
        )

    def cond_start():
        for slot in range(4):
            cond_copy(slot).start()

    def make_faces():
        wait_bytes(condrecv, cond_recv)
        shape = (own_y, own_y)
        eye = lax.broadcasted_iota(jnp.int32, shape, 0) == lax.broadcasted_iota(jnp.int32, shape, 1)
        lane = lax.broadcasted_iota(jnp.int32, (1, own_y), 1)

        def spread(row):
            full = jnp.where(eye, jnp.broadcast_to(row, shape), 0.0)
            return jnp.broadcast_to(jnp.sum(full, axis=1, keepdims=True), (own_y, 128))

        def pick(row, at):
            one = jnp.sum(jnp.where(lane == at, row, 0.0), axis=1, keepdims=True)
            return jnp.broadcast_to(one, (8, 128))

        def row_of(x, carry):
            cpad[x + 1, pl.ds(8, own_y), :] = spread(cond[pl.ds(x, 1), :])
            low = jnp.where(m == 0, 0.0, pick(condrecv[2, pl.ds(x, 1), :], own_y - 1))
            high = jnp.where(m == n_mem - 1, 0.0, pick(condrecv[3, pl.ds(x, 1), :], 0))
            cpad[x + 1, pl.ds(0, 8), :] = low
            cpad[x + 1, pl.ds(own_y + 8, 8), :] = high
            return carry

        lax.fori_loop(0, own_x, row_of, 0, unroll=4)
        first = jnp.where(g == 0, 0.0, condrecv[0, pl.ds(own_x - 1, 1), :])
        last = jnp.where(g == n_grp - 1, 0.0, condrecv[1, pl.ds(0, 1), :])
        cpad[0, pl.ds(8, own_y), :] = spread(first)
        cpad[own_x + 1, pl.ds(8, own_y), :] = spread(last)

        at_y = lax.broadcasted_iota(jnp.int32, (own_y + 8, 128), 0)
        inside = (at_y > 0) & (at_y < own_y)

        def face_x(x, carry):
            facex[x] = 0.5 * (cpad[x, pl.ds(8, own_y), :] + cpad[x + 1, pl.ds(8, own_y), :])
            return carry

        def face_y(x, carry):
            face = 0.5 * (cpad[x + 1, pl.ds(7, own_y + 8), :] + cpad[x + 1, pl.ds(8, own_y + 8), :])
            facey[x] = face
            inner_y[x] = jnp.where(inside, face, 0.0)
            return carry

        lax.fori_loop(0, own_x + 1, face_x, 0)
        lax.fori_loop(0, own_x, face_y, 0)

    def ex_copy(side):
        if side < 2:
            src = sol.at[1 if side == 0 else own_x, pl.ds(8, own_y), :]
            dst = sol.at[own_x + 1 if side == 0 else 0, pl.ds(8, own_y), :]
            device = {"grp": g_dn if side == 0 else g_up}
        else:
            src = esend.at[side - 2]
            dst = erecv.at[side - 2]
            device = {"mem": m_dn if side == 2 else m_up}
        return pltpu.make_async_remote_copy(
            src_ref=src, dst_ref=dst, send_sem=ex_send.at[side], recv_sem=ex_recv.at[side],
            device_id=device, device_id_type=MESH,
        )

    def sol_rows(i, lifted):
        co = dot(bcor[i], lifted)
        for j in range(2):
            value = fine[2 * i + j, pl.ds(OV, own_y), :] + co[j * own_y : (j + 1) * own_y]
            sol[2 * i + j + 1, pl.ds(8, own_y), :] = value

    def correct_edges(lifted):
        co = dot(bedge[...].astype(BF16), lifted)
        esend[0] = fine[:, OV, :] + co[:own_x]
        esend[1] = fine[:, OV + own_y - 1, :] + co[own_x:]
        sol_rows(0, lifted)
        sol_rows(own_x // 2 - 1, lifted)

    def ex_start():
        for side in range(4):
            ex_copy(side).start()

    def correct_inner(lifted):
        def step(i, carry):
            sol_rows(i, lifted)
            return carry

        lax.fori_loop(1, own_x // 2 - 1, step, 0, unroll=True)

    def zero_margin():
        zero = jnp.zeros((8, columns), F32)
        for x in range(own_x):
            sol[x + 1, pl.ds(0, 8), :] = zero
            sol[x + 1, pl.ds(own_y + 8, 8), :] = zero
            for it in range(2):
                res[it, x, pl.ds(0, 8), :] = zero
                res[it, x, pl.ds(own_y + 8, 8), :] = zero

    def thrice(v):
        return jnp.concatenate([v] * (columns // 128), axis=1)

    def inner_residual():
        def row(x, first, last):
            c = sol[x + 1, pl.ds(8, own_y), :]
            total = thrice(inner_y[x, pl.ds(1, own_y), :]) * (c - sol[x + 1, pl.ds(9, own_y), :])
            total += thrice(inner_y[x, pl.ds(0, own_y), :]) * (c - sol[x + 1, pl.ds(7, own_y), :])
            if not last:
                total += thrice(facex[x + 1]) * (c - sol[x + 2, pl.ds(8, own_y), :])
            if not first:
                total += thrice(facex[x]) * (c - sol[x, pl.ds(8, own_y), :])
            res[1, x, pl.ds(8, own_y), :] = res[0, x, pl.ds(8, own_y), :] - total

        def step(x, carry):
            row(x, False, False)
            return carry

        row(0, True, False)
        lax.fori_loop(1, own_x - 1, step, 0, unroll=2)
        row(own_x - 1, False, True)

    def outer_residual():
        for side in range(4):
            ex_copy(side).wait_recv()
        low_x = jnp.where(g == 0, 0.0, sol[0, pl.ds(8, own_y), :])
        high_x = jnp.where(g == n_grp - 1, 0.0, sol[own_x + 1, pl.ds(8, own_y), :])
        res[1, 0, pl.ds(8, own_y), :] -= thrice(facex[0]) * (sol[1, pl.ds(8, own_y), :] - low_x)
        res[1, own_x - 1, pl.ds(8, own_y), :] -= thrice(facex[own_x]) * (
            sol[own_x, pl.ds(8, own_y), :] - high_x
        )
        low_y = thrice(facey[:, 0, :]) * (esend[0] - jnp.where(m == 0, 0.0, erecv[1]))
        high_y = thrice(facey[:, own_y, :]) * (esend[1] - jnp.where(m == n_mem - 1, 0.0, erecv[0]))
        res[1, :, 8, :] -= low_y
        res[1, :, own_y + 7, :] -= high_y

    def finish_base():
        def step(x, carry):
            base_out[x] = sol[x + 1, pl.ds(8, own_y), :] + fine[x, pl.ds(OV, own_y), :]
            return carry

        lax.fori_loop(0, own_x, step, 0, unroll=2)

    blocks = mid // chunk
    prepare_basis()
    zero_margin()
    load_rhs.wait()
    restrict(0)
    load_cond.wait()
    pl.semaphore_wait(barrier, greets)
    cond_start()
    gather_start(0)
    each_grp(lambda d: c_copy(d).start())
    c_local.start()
    pack_x(0)
    x_start(0)
    pack_y(0)
    corner_start(0)
    assemble(0)
    load_inv.wait()
    select_x()
    select_y(0, 2)
    gather_forward(0, 0, (1, 3))
    y_start(0)
    gather_forward(0, 0, (2,))
    gather_forward(0, 1, (1, 3, 2))
    gather_forward(0, 2, (1, 3, 2))
    make_faces()
    select_y(2, blocks)
    wait_bytes(cblk.at[pl.ds(0, (n_grp - 1) * modes), :], c_recv)
    c_local.wait()
    csplit[0], csplit[1] = split(cblk[...])
    coarse_step(0, 0)
    coarse_step(0, 1)
    pair_step(0, 0)
    coarse_step(0, 2)
    pair_step(0, 1)
    pair_step(0, 2)
    fine_inner(0, blocks)
    finish_y(0)
    finish_x(0)
    fine_outer(0)
    lifted = lift(0)
    correct_edges(lifted)
    ex_start()
    correct_inner(lifted)
    inner_residual()

    outer_residual()
    pack_x(1)
    x_start(1)
    restrict(1)
    gather_start(1)
    pack_y(1)
    corner_start(1)
    assemble(1)
    gather_forward(1, 0, (1, 3))
    y_start(1)
    gather_forward(1, 0, (2,))
    gather_forward(1, 1, (1, 3, 2))
    gather_forward(1, 2, (1, 3, 2))
    fine_inner(0, 4)
    coarse_step(1, 0)
    coarse_step(1, 1)
    pair_step(1, 0)
    coarse_step(1, 2)
    pair_step(1, 1)
    pair_step(1, 2)
    fine_inner(4, blocks)
    finish_y(1)
    finish_x(1)
    fine_outer(1)
    finish_base()
    lifted_out[...] = lift(1)

    wait_bytes(cblk.at[pl.ds(0, (n_grp - 1) * modes), :], c_send)
    wait_bytes(condrecv, cond_send)
    for side in range(4):
        ex_copy(side).wait_send()
    for it in range(2):
        wait_bytes(rblk.at[it, :, pl.ds(0, (NZ - 1) * modes), :], az_send.at[it])
        wait_bytes(rblk.at[it, :, pl.ds(0, (n_y - 1) * NZ * modes), :], ay_send.at[it])
        wait_bytes(qbuf.at[it, :, pl.ds(1, n_pair - 1)], rs_send.at[it])
        for c in range(chunks):
            pair_copy(it, c).wait_send()
        for side in range(2):
            y_copy(it, side).wait_send()
            x_copy(it, side).wait_send()
            for y_side in range(2):
                corner_copy(it, side, y_side).wait_send()


def tail_kernel(base, lifted, bcor, out_hbm, outbuf, out_sem):
    pairs, own_y = base.shape[0] // 2, base.shape[1]
    per = 3

    def store(i):
        rows = pl.ds(2 * per * i, 2 * per)
        return pltpu.make_async_copy(outbuf.at[rows], out_hbm.at[rows], out_sem.at[i])

    for i in range(pairs // per):
        for k in range(per * i, per * i + per):
            co = dot(bcor[k], lifted[...])
            for j in range(2):
                outbuf[2 * k + j] = base[2 * k + j] + co[j * own_y : (j + 1) * own_y]
        store(i).start()
    for i in range(pairs // per):
        store(i).wait()


def on_device(rhs, conductivity, local_inverse, coarse_basis, coarse_inverse):
    own_x, own_y, columns = rhs.shape
    modes = coarse_basis.shape[2]
    n_grp, n_mem = lax.axis_size("grp"), lax.axis_size("mem")
    n_y = n_mem // NZ
    chunks = columns // LANES
    span_x, span_y = own_x + 2 * OV, own_y + 2 * OV
    basis_t = jnp.transpose(coarse_basis, (0, 2, 1))
    arrays = (rhs, conductivity, local_inverse, basis_t, coarse_inverse)
    hbm = pl.BlockSpec(memory_space=pltpu.HBM)
    vmem = pl.BlockSpec(memory_space=pltpu.VMEM)
    dma = pltpu.SemaphoreType.DMA
    scratch = [
        pltpu.VMEM((own_x, own_y), F32),
        pltpu.VMEM((own_x, modes, own_y), F32),
        pltpu.VMEM((own_x * span_y, span_x * span_y), BF16),
        pltpu.VMEM((2, own_x, own_y + 16, columns), F32),
        pltpu.VMEM((own_x * span_y, columns), BF16),
        pltpu.VMEM((2, 2 * OV * (span_y + own_x), columns), BF16),
        pltpu.VMEM((own_x * span_y, 2 * OV * (span_y + own_x)), BF16),
        pltpu.VMEM((own_x * span_y, 2 * OV * own_x), BF16),
        pltpu.VMEM((own_x, span_y, columns), F32),
        pltpu.VMEM((own_x + 2, own_y + 16, columns), F32),
        pltpu.VMEM((own_x + 2, own_y + 16, 128), F32),
        pltpu.VMEM((own_x + 1, own_y, 128), F32),
        pltpu.VMEM((own_x, own_y + 8, 128), F32),
        pltpu.VMEM((own_x, own_y + 8, 128), F32),
        pltpu.VMEM((own_x // 2, 2 * modes, 2 * own_y), BF16),
        pltpu.VMEM((own_x // 2, 2 * own_y, 3 * modes), BF16),
        pltpu.VMEM((2 * own_x, 3 * modes), F32),
        pltpu.VMEM((2, chunks, n_mem * modes, LANES), F32),
        pltpu.VMEM((n_grp * modes, n_mem * modes), F32),
        pltpu.VMEM((2, n_grp * modes, n_mem * modes), BF16),
        pltpu.VMEM((2, chunks, n_grp // 2, 2, modes, LANES), F32),
        pltpu.VMEM((2, chunks, n_grp // 2, modes, LANES), F32),
        pltpu.VMEM((2, chunks, n_grp // 2, modes, LANES), F32),
        pltpu.VMEM((2, chunks, n_grp // 2, modes, LANES), F32),
        pltpu.VMEM((2, 2, own_x * OV, columns), BF16),
        pltpu.VMEM((2, 2, OV * own_y, columns), BF16),
        pltpu.VMEM((2, own_x, columns), F32),
        pltpu.VMEM((2, own_x, columns), F32),
        pltpu.VMEM((4, own_x, own_y), F32),
        dma((4,)), dma,
        dma, dma, dma, dma,
        dma((2,)), dma((2, chunks, NZ)), dma((2,)), dma((2, chunks)),
        dma((2, chunks)), dma((2, chunks)), dma((2,)), dma((2, chunks)),
        dma((2, 2)), dma((2, 2)), dma((2, 2)), dma((2, 2)), dma((2, 2, 2)), dma((2, 2, 2)),
        dma((4,)), dma((4,)),
    ]
    base, lifted, bcor = pl.pallas_call(
        functools.partial(kernel, n_grp, n_mem, own_x, own_y),
        out_shape=(
            jax.ShapeDtypeStruct(rhs.shape, F32),
            jax.ShapeDtypeStruct((3 * modes, columns), BF16),
            jax.ShapeDtypeStruct((own_x // 2, 2 * own_y, 3 * modes), BF16),
        ),
        in_specs=[hbm] * 5,
        out_specs=(vmem, vmem, vmem),
        scratch_shapes=scratch,
        compiler_params=pltpu.CompilerParams(
            collective_id=0, has_side_effects=True, vmem_limit_bytes=44 * 1024 * 1024
        ),
    )(*(pltpu.with_memory_space_constraint(v, pltpu.HBM) for v in arrays))
    return pl.pallas_call(
        tail_kernel,
        out_shape=jax.ShapeDtypeStruct(rhs.shape, F32),
        in_specs=[vmem, vmem, vmem],
        out_specs=hbm,
        scratch_shapes=[pltpu.VMEM(rhs.shape, F32), dma((own_x // 6,))],
        compiler_params=pltpu.CompilerParams(vmem_limit_bytes=16 * 1024 * 1024),
    )(base, lifted, bcor)


def solution(mesh):
    placed = (
        P("grp", "mem", None),
        P("grp", "mem"),
        P(("grp", "mem"), None),
        P("grp", "mem", None),
        P(("grp", "mem"), None),
    )
    return jax.shard_map(
        on_device, mesh=mesh, in_specs=placed, out_specs=P("grp", "mem", None), check_vma=False
    )
```

```python
import functools
import jax
import jax.numpy as jnp
from jax import lax
from jax.experimental import pallas as pl
from jax.experimental.pallas import tpu as pltpu
from jax.sharding import PartitionSpec as P

OV = 4
LANES = 128
NZ = 4
MESH = pl.DeviceIdType.MESH
F32 = jnp.float32
BF16 = jnp.bfloat16


def split(v):
    hi = v.astype(BF16)
    lo = (v - hi.astype(F32)).astype(BF16)
    return hi, lo


def dot(a, b):
    return jnp.dot(a, b, preferred_element_type=F32)


def kernel(
    n_grp, n_mem, own_x, own_y,
    rhs_hbm, cond_hbm, linv_hbm, basis_hbm, cinv_hbm,
    base_out, lifted_out, bcor_out,
    cond, basis_t, lbuf, res, win, wmar, lmar, ysel, fine, sol, cpad, facex, facey, inner_y,
    bres, bcor, bedge, rblk, cblk, csplit, part, pairbuf, sumbuf, qbuf,
    ysend, xsend, esend, erecv, condrecv,
    in_sem, cloc_sem,
    c_send, c_recv, cond_send, cond_recv,
    az_send, az_recv, ay_send, ay_recv, pr_send, pr_recv, rs_send, rs_recv,
    yh_send, yh_recv, xh_send, xh_recv, co_send, co_recv, ex_send, ex_recv,
):
    g = lax.axis_index("grp")
    m = lax.axis_index("mem")
    n_y = n_mem // NZ
    my = m // NZ
    mz = lax.rem(m, NZ)
    n_pair = n_grp // 2
    pair = g // 2
    core = lax.rem(g, 2)
    span_y = own_y + 2 * OV
    columns = rhs_hbm.shape[2]
    modes = basis_hbm.shape[1]
    chunks = columns // LANES
    edge = OV * span_y
    y_margin = own_x * OV

    def y_rows(side):
        return pl.ds(2 * edge + side * y_margin, y_margin)

    def x_rows(side):
        return pl.ds(side * edge, OV * own_y)

    mid = own_x * span_y
    g_up = lax.rem(g + 1, n_grp)
    g_dn = lax.rem(g + n_grp - 1, n_grp)
    m_up = lax.rem(m + 1, n_mem)
    m_dn = lax.rem(m + n_mem - 1, n_mem)

    has_x = (g > 0, g < n_grp - 1)
    has_y = (m > 0, m < n_mem - 1)

    def only(condition, action):
        pl.when(condition)(action)

    def z_peer(d):
        return my * NZ + lax.rem(mz + d, NZ)

    def y_peer(d):
        return lax.rem(my + d, n_y) * NZ + mz

    def wait_bytes(ref, sem):
        pltpu.make_async_copy(ref, ref, sem).wait()

    load_rhs = pltpu.make_async_copy(rhs_hbm, res.at[0, :, pl.ds(8, own_y), :], in_sem.at[0])
    load_inv = pltpu.make_async_copy(linv_hbm.at[pl.ds(edge, mid), :], lbuf, in_sem.at[1])
    load_cond = pltpu.make_async_copy(cond_hbm, cond, in_sem.at[2])
    load_basis = pltpu.make_async_copy(basis_hbm, basis_t, in_sem.at[3])
    load_basis.start()
    load_rhs.start()
    load_cond.start()
    load_inv.start()

    barrier = pltpu.get_barrier_semaphore()

    def greet_grp(d, carry):
        pl.semaphore_signal(
            barrier, inc=1, device_id={"grp": lax.rem(g + d, n_grp)}, device_id_type=MESH
        )
        return carry

    lax.fori_loop(1, n_grp, greet_grp, 0)
    greets = n_grp - 1
    for peer in [z_peer(d) for d in range(1, NZ)] + [y_peer(d) for d in range(1, n_y)] + [m_up, m_dn]:
        pl.semaphore_signal(barrier, inc=1, device_id={"mem": peer}, device_id_type=MESH)
        greets += 1
    for g_side in (g_dn, g_up):
        for m_side in (m_dn, m_up):
            pl.semaphore_signal(
                barrier, inc=1, device_id={"grp": g_side, "mem": m_side}, device_id_type=MESH
            )
            greets += 1

    def wide_basis(i):
        return split(jnp.concatenate([basis_t[2 * i], basis_t[2 * i + 1]], axis=1))

    load_basis.wait()
    for i in range(own_x // 2):
        bres[i] = jnp.concatenate(wide_basis(i), axis=0)

    def prepare_basis():
        for i in range(own_x // 2):
            hi, lo = (v.astype(F32) for v in wide_basis(i))
            tall = jnp.transpose(jnp.concatenate([hi, lo, hi], axis=0))
            bcor[i] = tall.astype(BF16)
            for j in range(2):
                x = 2 * i + j
                bedge[pl.ds(x, 1), :] = tall[j * own_y : j * own_y + 1]
                bedge[pl.ds(own_x + x, 1), :] = tall[(j + 1) * own_y - 1 : (j + 1) * own_y]
        bcor_out[...] = bcor[...]

    own_rows = pl.ds(pl.multiple_of(m * modes, modes), modes)

    def restrict(it):
        def step(i, total):
            pair = res[it, pl.ds(2 * i, 2), pl.ds(8, own_y), :].reshape(2 * own_y, columns)
            hi, lo = split(pair)
            both = dot(bres[i], hi)
            return total + both[:modes] + both[modes:] + dot(bres[i, pl.ds(0, modes), :], lo)

        total = lax.fori_loop(0, own_x // 2, step, jnp.zeros((modes, columns), F32), unroll=True)
        for c in range(chunks):
            rblk[it, c, own_rows, :] = total[:, c * LANES : (c + 1) * LANES]

    low_half = lax.broadcasted_iota(jnp.int32, (own_x // 2, 8, columns), 1) < OV

    def flip(v):
        return pltpu.roll(v, OV, 1)

    def pack_y(it):
        left = res[it, :, pl.ds(8, 8), :].reshape(own_x // 2, 2, 8, columns)
        right = res[it, :, pl.ds(own_y, 8), :].reshape(own_x // 2, 2, 8, columns)
        lo_side = jnp.where(low_half, left[:, 0], flip(left[:, 1]))
        hi_side = jnp.where(low_half, flip(right[:, 0]), right[:, 1])
        ysend[it, 0] = lo_side.reshape(own_x * OV, columns).astype(BF16)
        ysend[it, 1] = hi_side.reshape(own_x * OV, columns).astype(BF16)

    def y_copy(it, side):
        return pltpu.make_async_remote_copy(
            src_ref=ysend.at[it, side],
            dst_ref=wmar.at[it, y_rows(1 - side), :],
            send_sem=yh_send.at[it, side],
            recv_sem=yh_recv.at[it, 1 - side],
            device_id={"mem": m_dn if side == 0 else m_up},
            device_id_type=MESH,
        )

    def finish_y(it):
        for side in range(2):
            only(has_y[side], lambda side=side: y_copy(it, 1 - side).wait_recv())

            @pl.when(jnp.logical_not(has_y[side]))
            def _(side=side):
                wmar[it, y_rows(side), :] = jnp.zeros((y_margin, columns), BF16)

    def assemble(it):
        def row(x, carry):
            win[pl.ds(pl.multiple_of(x * span_y, span_y), span_y), :] = res[
                it, x, pl.ds(8 - OV, span_y), :
            ].astype(BF16)
            return carry

        lax.fori_loop(0, own_x, row, 0, unroll=4)

    def pack_x(it):
        for side, first in ((0, 0), (1, own_x - OV)):
            rows = res[it, pl.ds(first, OV), pl.ds(8, own_y), :]
            xsend[it, side] = rows.reshape(OV * own_y, columns).astype(BF16)

    def x_copy(it, side):
        return pltpu.make_async_remote_copy(
            src_ref=xsend.at[it, side],
            dst_ref=wmar.at[it, x_rows(1 - side), :],
            send_sem=xh_send.at[it, side],
            recv_sem=xh_recv.at[it, 1 - side],
            device_id={"grp": g_dn if side == 0 else g_up},
            device_id_type=MESH,
        )

    def corner_copy(it, side, y_side):
        first = 0 if side == 0 else (own_x - OV) * OV
        lands = (1 - side) * edge + OV * own_y + (1 - y_side) * OV * OV
        return pltpu.make_async_remote_copy(
            src_ref=ysend.at[it, y_side, pl.ds(first, OV * OV), :],
            dst_ref=wmar.at[it, pl.ds(lands, OV * OV), :],
            send_sem=co_send.at[it, side, y_side],
            recv_sem=co_recv.at[it, 1 - side, 1 - y_side],
            device_id={
                "grp": g_dn if side == 0 else g_up,
                "mem": m_dn if y_side == 0 else m_up,
            },
            device_id_type=MESH,
        )

    def corner_start(it):
        for side in range(2):
            for y_side in range(2):
                only(has_x[side] & has_y[y_side], corner_copy(it, side, y_side).start)

    def finish_x(it):
        for side in range(2):
            only(has_x[side], lambda side=side: x_copy(it, 1 - side).wait_recv())

            @pl.when(jnp.logical_not(has_x[side]))
            def _(side=side):
                wmar[it, x_rows(side), :] = jnp.zeros((OV * own_y, columns), BF16)

            for y_side in range(2):
                both = has_x[side] & has_y[y_side]
                only(both, lambda side=side, y_side=y_side: corner_copy(it, 1 - side, 1 - y_side).wait_recv())

                @pl.when(jnp.logical_not(both))
                def _(side=side, y_side=y_side):
                    lands = side * edge + OV * own_y + y_side * OV * OV
                    wmar[it, pl.ds(lands, OV * OV), :] = jnp.zeros((OV * OV, columns), BF16)

    chunk = OV * span_y

    def selector(shape, column_of):
        out = lax.broadcasted_iota(jnp.int32, shape, 1)
        into = lax.broadcasted_iota(jnp.int32, shape, 0)
        return jnp.where(into == column_of(out), 1.0, 0.0).astype(BF16)

    def x_column(n):
        row = sum((n >= own_y * k).astype(jnp.int32) for k in range(1, OV))
        corner = n - OV * own_y
        far = (corner >= OV * OV).astype(jnp.int32)
        corner = corner - far * OV * OV
        inside = row * (span_y - own_y) + n + OV
        outside = (corner // OV) * span_y + corner % OV + far * (span_y - OV)
        return jnp.where(n < OV * own_y, inside, outside)

    def y_column(n):
        far = (n >= y_margin).astype(jnp.int32)
        n = n - far * y_margin
        return (n // OV) * span_y + n % OV + far * (span_y - OV)

    def select_x():
        pick = selector((edge, edge), x_column)

        def step(i, carry):
            rows = pl.ds(pl.multiple_of(i * chunk, chunk), chunk)
            for side, first in ((0, 0), (1, edge + mid)):
                got = dot(lbuf[rows, pl.ds(first, edge)], pick)
                lmar[rows, pl.ds(side * edge, edge)] = got.astype(BF16)
            return carry

        lax.fori_loop(0, mid // chunk, step, 0)

    def select_y(first, last):
        if first == 0:
            ysel[...] = selector((mid, 2 * y_margin), y_column)

        def step(i, carry):
            rows = pl.ds(pl.multiple_of(i * chunk, chunk), chunk)
            got = dot(lbuf[rows, pl.ds(edge, mid)], ysel[...])
            lmar[rows, pl.ds(2 * edge, 2 * y_margin)] = got.astype(BF16)
            return carry

        lax.fori_loop(first, last, step, 0)

    def fine_inner(first, last):
        def step(i, carry):
            rows = pl.ds(pl.multiple_of(i * chunk, chunk), chunk)
            got = dot(lbuf[rows, pl.ds(edge, mid)], win[...])
            fine[pl.ds(i * OV, OV)] = got.reshape(OV, span_y, columns)
            return carry

        lax.fori_loop(first, last, step, 0)

    def fine_outer(it):
        def step(i, carry):
            rows = pl.ds(pl.multiple_of(i * chunk, chunk), chunk)
            got = dot(lmar[rows, :], wmar[it])
            fine[pl.ds(i * OV, OV)] += got.reshape(OV, span_y, columns)
            return carry

        lax.fori_loop(0, own_x // OV, step, 0)

    def z_copy(it, c, d):
        return pltpu.make_async_remote_copy(
            src_ref=rblk.at[it, c, own_rows, :], dst_ref=rblk.at[it, c, own_rows, :],
            send_sem=az_send.at[it], recv_sem=az_recv.at[it, c, d],
            device_id={"mem": z_peer(d)}, device_id_type=MESH,
        )

    def y_forward(it, c, d, src_d):
        block = my * NZ + lax.rem(mz + NZ - src_d, NZ)
        rows = pl.ds(pl.multiple_of(block * modes, modes), modes)
        return pltpu.make_async_remote_copy(
            src_ref=rblk.at[it, c, rows, :], dst_ref=rblk.at[it, c, rows, :],
            send_sem=ay_send.at[it], recv_sem=ay_recv.at[it, c],
            device_id={"mem": y_peer(d)}, device_id_type=MESH,
        )

    def gather_start(it):
        for c in range(chunks):
            for d in (2, 1, 3):
                z_copy(it, c, d).start()
            for d in range(1, n_y):
                y_forward(it, c, d, 0).start()

    def gather_forward(it, c, sources):
        for src_d in sources:
            z_copy(it, c, src_d).wait_recv()
            for d in range(1, n_y):
                y_forward(it, c, d, src_d).start()

    def gather_finish(it, c):
        wait_bytes(rblk.at[it, c, pl.ds(0, (n_y - 1) * NZ * modes), :], ay_recv.at[it, c])

    def c_copy(d):
        dest = lax.rem(g + d, n_grp)
        return pltpu.make_async_remote_copy(
            src_ref=cinv_hbm.at[:, pl.ds(pl.multiple_of(dest * n_mem * modes, n_mem * modes), n_mem * modes)],
            dst_ref=cblk.at[pl.ds(pl.multiple_of(g * modes, modes), modes), :],
            send_sem=c_send, recv_sem=c_recv,
            device_id={"grp": dest}, device_id_type=MESH,
        )

    c_local = pltpu.make_async_copy(
        cinv_hbm.at[:, pl.ds(pl.multiple_of(g * n_mem * modes, n_mem * modes), n_mem * modes)],
        cblk.at[pl.ds(pl.multiple_of(g * modes, modes), modes), :],
        cloc_sem,
    )

    def each_grp(action):
        def body(d, carry):
            action(d)
            return carry

        lax.fori_loop(1, n_grp, body, 0)

    def coarse_multiply(it, c):
        hi, lo = split(rblk[it, c])
        both = jnp.concatenate([hi, lo], axis=1)

        def step(i, carry):
            rows = pl.ds(pl.multiple_of(i * 128, 128), 128)
            two = dot(csplit[0, rows, :], both)
            got = two[:, :LANES] + (two[:, LANES:] + dot(csplit[1, rows, :], hi))
            part[it, c, pl.ds(i * 4, 4)] = got.reshape(4, 2, modes, LANES)
            return carry

        lax.fori_loop(0, n_grp * modes // 128, step, 0, unroll=True)

    def pair_copy(it, c):
        return pltpu.make_async_remote_copy(
            src_ref=part.at[it, c, :, 1 - core], dst_ref=pairbuf.at[it, c],
            send_sem=pr_send.at[it, c], recv_sem=pr_recv.at[it, c],
            device_id={"grp": 2 * pair + 1 - core}, device_id_type=MESH,
        )

    def rs_copy(it, c, d):
        dest = lax.rem(pair + d, n_pair)
        return pltpu.make_async_remote_copy(
            src_ref=sumbuf.at[it, c, dest], dst_ref=qbuf.at[it, c, d],
            send_sem=rs_send.at[it], recv_sem=rs_recv.at[it, c],
            device_id={"grp": 2 * dest + core}, device_id_type=MESH,
        )

    def pair_step(it, c):
        pair_copy(it, c).wait_recv()
        sumbuf[it, c] = part[it, c, :, core] + pairbuf[it, c]
        for d in range(1, n_pair):
            rs_copy(it, c, d).start()

    def lift(it):
        pieces = []
        for c in range(chunks):
            wait_bytes(qbuf.at[it, c, pl.ds(1, n_pair - 1)], rs_recv.at[it, c])
            total = sumbuf[it, c, pair]
            for d in range(1, n_pair):
                total = total + qbuf[it, c, d]
            pieces.append(total)
        hi, lo = split(jnp.concatenate(pieces, axis=1))
        return jnp.concatenate([hi.astype(F32), hi.astype(F32), lo.astype(F32)], axis=0).astype(BF16)

    def coarse_step(it, c):
        gather_finish(it, c)
        coarse_multiply(it, c)
        pair_copy(it, c).start()

    def drain(it):
        wait_bytes(rblk.at[it, :, pl.ds(0, (NZ - 1) * modes), :], az_send.at[it])
        wait_bytes(rblk.at[it, :, pl.ds(0, (n_y - 1) * NZ * modes), :], ay_send.at[it])
        for c in range(chunks):
            pair_copy(it, c).wait_send()
        for side in range(2):
            only(has_y[side], lambda side=side: y_copy(it, side).wait_send())
            only(has_x[side], lambda side=side: x_copy(it, side).wait_send())
            for y_side in range(2):
                only(
                    has_x[side] & has_y[y_side],
                    lambda side=side, y_side=y_side: corner_copy(it, side, y_side).wait_send(),
                )
        if it == 0:
            wait_bytes(cblk.at[pl.ds(0, (n_grp - 1) * modes), :], c_send)
            for slot in range(4):
                only((has_x + has_y)[slot ^ 1], lambda slot=slot: cond_copy(slot).wait_send())
                only((has_x + has_y)[slot], lambda slot=slot: ex_copy(slot).wait_send())
            wait_bytes(sumbuf.at[0, :, pl.ds(1, n_pair - 1)], rs_send.at[0])

    def y_start(it):
        for side in range(2):
            only(has_y[side], y_copy(it, side).start)

    far_x = (g == n_grp // 2, g == n_grp // 2 - 1)

    def x_start(it, far):
        for side in range(2):
            there = far_x[side] if far else has_x[side] & jnp.logical_not(far_x[side])
            only(there, x_copy(it, side).start)

    def cond_copy(slot):
        if slot < 2:
            device = {"grp": g_up if slot == 0 else g_dn}
        else:
            device = {"mem": m_up if slot == 2 else m_dn}
        return pltpu.make_async_remote_copy(
            src_ref=cond, dst_ref=condrecv.at[slot],
            send_sem=cond_send.at[slot], recv_sem=cond_recv.at[slot],
            device_id=device, device_id_type=MESH,
        )

    def cond_start():
        for slot in range(4):
            only((has_x + has_y)[slot ^ 1], cond_copy(slot).start)

    def make_faces():
        for slot in range(4):
            only((has_x + has_y)[slot], lambda slot=slot: cond_copy(slot).wait_recv())
        shape = (own_y, own_y)
        eye = lax.broadcasted_iota(jnp.int32, shape, 0) == lax.broadcasted_iota(jnp.int32, shape, 1)
        lane = lax.broadcasted_iota(jnp.int32, (1, own_y), 1)

        def spread(row):
            full = jnp.where(eye, jnp.broadcast_to(row, shape), 0.0)
            return jnp.broadcast_to(jnp.sum(full, axis=1, keepdims=True), (own_y, 128))

        def pick(row, at):
            one = jnp.sum(jnp.where(lane == at, row, 0.0), axis=1, keepdims=True)
            return jnp.broadcast_to(one, (8, 128))

        def row_of(x, carry):
            cpad[x + 1, pl.ds(8, own_y), :] = spread(cond[pl.ds(x, 1), :])
            low = jnp.where(m == 0, 0.0, pick(condrecv[2, pl.ds(x, 1), :], own_y - 1))
            high = jnp.where(m == n_mem - 1, 0.0, pick(condrecv[3, pl.ds(x, 1), :], 0))
            cpad[x + 1, pl.ds(0, 8), :] = low
            cpad[x + 1, pl.ds(own_y + 8, 8), :] = high
            return carry

        lax.fori_loop(0, own_x, row_of, 0, unroll=4)
        first = jnp.where(g == 0, 0.0, condrecv[0, pl.ds(own_x - 1, 1), :])
        last = jnp.where(g == n_grp - 1, 0.0, condrecv[1, pl.ds(0, 1), :])
        cpad[0, pl.ds(8, own_y), :] = spread(first)
        cpad[own_x + 1, pl.ds(8, own_y), :] = spread(last)

        at_y = lax.broadcasted_iota(jnp.int32, (own_y + 8, 128), 0)
        inside = (at_y > 0) & (at_y < own_y)

        def face_x(x, carry):
            facex[x] = 0.5 * (cpad[x, pl.ds(8, own_y), :] + cpad[x + 1, pl.ds(8, own_y), :])
            return carry

        def face_y(x, carry):
            face = 0.5 * (cpad[x + 1, pl.ds(7, own_y + 8), :] + cpad[x + 1, pl.ds(8, own_y + 8), :])
            facey[x] = face
            inner_y[x] = jnp.where(inside, face, 0.0)
            return carry

        lax.fori_loop(0, own_x + 1, face_x, 0)
        lax.fori_loop(0, own_x, face_y, 0)

    def ex_copy(side):
        if side < 2:
            src = sol.at[1 if side == 0 else own_x, pl.ds(8, own_y), :]
            dst = sol.at[own_x + 1 if side == 0 else 0, pl.ds(8, own_y), :]
            device = {"grp": g_dn if side == 0 else g_up}
        else:
            src = esend.at[side - 2]
            dst = erecv.at[side - 2]
            device = {"mem": m_dn if side == 2 else m_up}
        return pltpu.make_async_remote_copy(
            src_ref=src, dst_ref=dst, send_sem=ex_send.at[side], recv_sem=ex_recv.at[side],
            device_id=device, device_id_type=MESH,
        )

    def sol_rows(i, lifted):
        co = dot(bcor[i], lifted)
        for j in range(2):
            value = fine[2 * i + j, pl.ds(OV, own_y), :] + co[j * own_y : (j + 1) * own_y]
            sol[2 * i + j + 1, pl.ds(8, own_y), :] = value

    def correct_edges(lifted):
        co = dot(bedge[...].astype(BF16), lifted)
        esend[0] = fine[:, OV, :] + co[:own_x]
        esend[1] = fine[:, OV + own_y - 1, :] + co[own_x:]
        sol_rows(0, lifted)
        sol_rows(own_x // 2 - 1, lifted)

    def ex_start():
        for side in range(4):
            only((has_x + has_y)[side], ex_copy(side).start)

    def correct_inner(lifted):
        def step(i, carry):
            sol_rows(i, lifted)
            return carry

        lax.fori_loop(1, own_x // 2 - 1, step, 0, unroll=True)

    def zero_margin():
        zero = jnp.zeros((8, columns), F32)
        for x in range(own_x):
            sol[x + 1, pl.ds(0, 8), :] = zero
            sol[x + 1, pl.ds(own_y + 8, 8), :] = zero
            for it in range(2):
                res[it, x, pl.ds(0, 8), :] = zero
                res[it, x, pl.ds(own_y + 8, 8), :] = zero

    def thrice(v):
        return jnp.concatenate([v] * (columns // 128), axis=1)

    def inner_residual():
        def row(x, first, last):
            c = sol[x + 1, pl.ds(8, own_y), :]
            total = thrice(inner_y[x, pl.ds(1, own_y), :]) * (c - sol[x + 1, pl.ds(9, own_y), :])
            total += thrice(inner_y[x, pl.ds(0, own_y), :]) * (c - sol[x + 1, pl.ds(7, own_y), :])
            if not last:
                total += thrice(facex[x + 1]) * (c - sol[x + 2, pl.ds(8, own_y), :])
            if not first:
                total += thrice(facex[x]) * (c - sol[x, pl.ds(8, own_y), :])
            res[1, x, pl.ds(8, own_y), :] = res[0, x, pl.ds(8, own_y), :] - total

        def step(x, carry):
            row(x, False, False)
            return carry

        row(0, True, False)
        lax.fori_loop(1, own_x - 1, step, 0, unroll=2)
        row(own_x - 1, False, True)

    def outer_residual():
        for side in range(4):
            only((has_x + has_y)[side ^ 1], lambda side=side: ex_copy(side).wait_recv())
        low_x = jnp.where(g == 0, 0.0, sol[0, pl.ds(8, own_y), :])
        high_x = jnp.where(g == n_grp - 1, 0.0, sol[own_x + 1, pl.ds(8, own_y), :])
        res[1, 0, pl.ds(8, own_y), :] -= thrice(facex[0]) * (sol[1, pl.ds(8, own_y), :] - low_x)
        res[1, own_x - 1, pl.ds(8, own_y), :] -= thrice(facex[own_x]) * (
            sol[own_x, pl.ds(8, own_y), :] - high_x
        )
        low_y = thrice(facey[:, 0, :]) * (esend[0] - jnp.where(m == 0, 0.0, erecv[1]))
        high_y = thrice(facey[:, own_y, :]) * (esend[1] - jnp.where(m == n_mem - 1, 0.0, erecv[0]))
        res[1, :, 8, :] -= low_y
        res[1, :, own_y + 7, :] -= high_y

    def finish_base():
        def step(x, carry):
            base_out[x] = sol[x + 1, pl.ds(8, own_y), :] + fine[x, pl.ds(OV, own_y), :]
            return carry

        lax.fori_loop(0, own_x, step, 0, unroll=2)

    blocks = mid // chunk
    prepare_basis()
    zero_margin()
    load_rhs.wait()
    restrict(0)
    load_cond.wait()
    pl.semaphore_wait(barrier, greets)
    gather_start(0)
    cond_start()
    each_grp(lambda d: c_copy(d).start())
    c_local.start()
    pack_x(0)
    pack_y(0)
    assemble(0)
    load_inv.wait()
    select_x()
    fine_inner(0, 2)
    gather_forward(0, 0, (1, 3, 2))
    gather_forward(0, 1, (1, 3, 2))
    gather_forward(0, 2, (1, 3, 2))
    x_start(0, True)
    x_start(0, False)
    corner_start(0)
    fine_inner(2, 4)
    y_start(0)
    fine_inner(4, blocks)
    wait_bytes(cblk.at[pl.ds(0, (n_grp - 1) * modes), :], c_recv)
    c_local.wait()
    csplit[0], csplit[1] = split(cblk[...])
    coarse_step(0, 0)
    coarse_step(0, 1)
    pair_step(0, 0)
    coarse_step(0, 2)
    pair_step(0, 1)
    pair_step(0, 2)
    select_y(0, blocks)
    finish_y(0)
    finish_x(0)
    fine_outer(0)
    lifted = lift(0)
    correct_edges(lifted)
    ex_start()
    make_faces()
    correct_inner(lifted)
    inner_residual()

    outer_residual()
    restrict(1)
    gather_start(1)
    pack_x(1)
    x_start(1, True)
    x_start(1, False)
    pack_y(1)
    corner_start(1)
    assemble(1)
    gather_forward(1, 0, (1, 3, 2))
    gather_forward(1, 1, (1, 3, 2))
    gather_forward(1, 2, (1, 3, 2))
    fine_inner(0, 2)
    y_start(1)
    fine_inner(2, 4)
    coarse_step(1, 0)
    coarse_step(1, 1)
    pair_step(1, 0)
    coarse_step(1, 2)
    pair_step(1, 1)
    pair_step(1, 2)
    fine_inner(4, blocks)
    finish_y(1)
    finish_x(1)
    fine_outer(1)
    finish_base()
    drain(0)
    drain(1)
    lifted_out[...] = lift(1)

    wait_bytes(sumbuf.at[1, :, pl.ds(1, n_pair - 1)], rs_send.at[1])


def tail_kernel(base, lifted, bcor, out_hbm, outbuf, out_sem):
    pairs, own_y = base.shape[0] // 2, base.shape[1]
    per = 3

    def store(i):
        rows = pl.ds(2 * per * i, 2 * per)
        return pltpu.make_async_copy(outbuf.at[rows], out_hbm.at[rows], out_sem.at[i])

    for i in range(pairs // per):
        for k in range(per * i, per * i + per):
            co = dot(bcor[k], lifted[...])
            for j in range(2):
                outbuf[2 * k + j] = base[2 * k + j] + co[j * own_y : (j + 1) * own_y]
        store(i).start()
    for i in range(pairs // per):
        store(i).wait()


def on_device(rhs, conductivity, local_inverse, coarse_basis, coarse_inverse):
    own_x, own_y, columns = rhs.shape
    modes = coarse_basis.shape[2]
    n_grp, n_mem = lax.axis_size("grp"), lax.axis_size("mem")
    n_y = n_mem // NZ
    chunks = columns // LANES
    span_x, span_y = own_x + 2 * OV, own_y + 2 * OV
    basis_t = jnp.transpose(coarse_basis, (0, 2, 1))
    arrays = (rhs, conductivity, local_inverse, basis_t, coarse_inverse)
    hbm = pl.BlockSpec(memory_space=pltpu.HBM)
    vmem = pl.BlockSpec(memory_space=pltpu.VMEM)
    dma = pltpu.SemaphoreType.DMA
    scratch = [
        pltpu.VMEM((own_x, own_y), F32),
        pltpu.VMEM((own_x, modes, own_y), F32),
        pltpu.VMEM((own_x * span_y, span_x * span_y), BF16),
        pltpu.VMEM((2, own_x, own_y + 16, columns), F32),
        pltpu.VMEM((own_x * span_y, columns), BF16),
        pltpu.VMEM((2, 2 * OV * (span_y + own_x), columns), BF16),
        pltpu.VMEM((own_x * span_y, 2 * OV * (span_y + own_x)), BF16),
        pltpu.VMEM((own_x * span_y, 2 * OV * own_x), BF16),
        pltpu.VMEM((own_x, span_y, columns), F32),
        pltpu.VMEM((own_x + 2, own_y + 16, columns), F32),
        pltpu.VMEM((own_x + 2, own_y + 16, 128), F32),
        pltpu.VMEM((own_x + 1, own_y, 128), F32),
        pltpu.VMEM((own_x, own_y + 8, 128), F32),
        pltpu.VMEM((own_x, own_y + 8, 128), F32),
        pltpu.VMEM((own_x // 2, 2 * modes, 2 * own_y), BF16),
        pltpu.VMEM((own_x // 2, 2 * own_y, 3 * modes), BF16),
        pltpu.VMEM((2 * own_x, 3 * modes), F32),
        pltpu.VMEM((2, chunks, n_mem * modes, LANES), F32),
        pltpu.VMEM((n_grp * modes, n_mem * modes), F32),
        pltpu.VMEM((2, n_grp * modes, n_mem * modes), BF16),
        pltpu.VMEM((2, chunks, n_grp // 2, 2, modes, LANES), F32),
        pltpu.VMEM((2, chunks, n_grp // 2, modes, LANES), F32),
        pltpu.VMEM((2, chunks, n_grp // 2, modes, LANES), F32),
        pltpu.VMEM((2, chunks, n_grp // 2, modes, LANES), F32),
        pltpu.VMEM((2, 2, own_x * OV, columns), BF16),
        pltpu.VMEM((2, 2, OV * own_y, columns), BF16),
        pltpu.VMEM((2, own_x, columns), F32),
        pltpu.VMEM((2, own_x, columns), F32),
        pltpu.VMEM((4, own_x, own_y), F32),
        dma((4,)), dma,
        dma, dma, dma((4,)), dma((4,)),
        dma((2,)), dma((2, chunks, NZ)), dma((2,)), dma((2, chunks)),
        dma((2, chunks)), dma((2, chunks)), dma((2,)), dma((2, chunks)),
        dma((2, 2)), dma((2, 2)), dma((2, 2)), dma((2, 2)), dma((2, 2, 2)), dma((2, 2, 2)),
        dma((4,)), dma((4,)),
    ]
    base, lifted, bcor = pl.pallas_call(
        functools.partial(kernel, n_grp, n_mem, own_x, own_y),
        out_shape=(
            jax.ShapeDtypeStruct(rhs.shape, F32),
            jax.ShapeDtypeStruct((3 * modes, columns), BF16),
            jax.ShapeDtypeStruct((own_x // 2, 2 * own_y, 3 * modes), BF16),
        ),
        in_specs=[hbm] * 5,
        out_specs=(vmem, vmem, vmem),
        scratch_shapes=scratch,
        compiler_params=pltpu.CompilerParams(
            collective_id=0, has_side_effects=True, vmem_limit_bytes=44 * 1024 * 1024
        ),
    )(*(pltpu.with_memory_space_constraint(v, pltpu.HBM) for v in arrays))
    return pl.pallas_call(
        tail_kernel,
        out_shape=jax.ShapeDtypeStruct(rhs.shape, F32),
        in_specs=[vmem, vmem, vmem],
        out_specs=hbm,
        scratch_shapes=[pltpu.VMEM(rhs.shape, F32), dma((own_x // 6,))],
        compiler_params=pltpu.CompilerParams(vmem_limit_bytes=16 * 1024 * 1024),
    )(base, lifted, bcor)


def solution(mesh):
    placed = (
        P("grp", "mem", None),
        P("grp", "mem"),
        P(("grp", "mem"), None),
        P("grp", "mem", None),
        P(("grp", "mem"), None),
    )
    return jax.shard_map(
        on_device, mesh=mesh, in_specs=placed, out_specs=P("grp", "mem", None), check_vma=False
    )
```

```python
import functools
import jax
import jax.numpy as jnp
from jax import lax
from jax.experimental import pallas as pl
from jax.experimental.pallas import tpu as pltpu
from jax.sharding import PartitionSpec as P

OV = 4
LANES = 128
NZ = 4
MESH = pl.DeviceIdType.MESH
F32 = jnp.float32
BF16 = jnp.bfloat16


def split(v):
    hi = v.astype(BF16)
    lo = (v - hi.astype(F32)).astype(BF16)
    return hi, lo


def dot(a, b):
    return jnp.dot(a, b, preferred_element_type=F32)


def kernel(
    n_grp, n_mem, own_x, own_y,
    rhs_hbm, cond_hbm, linv_hbm, basis_hbm, cinv_hbm,
    base_out, lifted_out, bcor_out,
    cond, basis_t, lbuf, res, win, wmar, lmar, ysel, fine, sol, cpad, facex, facey, inner_y,
    bres, bcor, bedge, brim, rblk, cblk, csplit, part, pairbuf, sumbuf, qbuf,
    ysend, xsend, esend, erecv, condrecv,
    in_sem, rhs_sem, cloc_sem,
    c_send, c_recv, cond_send, cond_recv,
    az_send, az_recv, ay_send, ay_recv, pr_send, pr_recv, rs_send, rs_recv,
    yh_send, yh_recv, xh_send, xh_recv, co_send, co_recv, ex_send, ex_recv,
):
    g = lax.axis_index("grp")
    m = lax.axis_index("mem")
    n_y = n_mem // NZ
    my = m // NZ
    mz = lax.rem(m, NZ)
    n_pair = n_grp // 2
    pair = g // 2
    core = lax.rem(g, 2)
    span_y = own_y + 2 * OV
    columns = rhs_hbm.shape[2]
    modes = basis_hbm.shape[1]
    chunks = columns // LANES
    edge = OV * span_y
    y_margin = own_x * OV

    def y_rows(side):
        return pl.ds(2 * edge + side * y_margin, y_margin)

    def x_rows(side):
        return pl.ds(side * edge, OV * own_y)

    mid = own_x * span_y
    g_up = lax.rem(g + 1, n_grp)
    g_dn = lax.rem(g + n_grp - 1, n_grp)
    m_up = lax.rem(m + 1, n_mem)
    m_dn = lax.rem(m + n_mem - 1, n_mem)

    has_x = (g > 0, g < n_grp - 1)
    has_y = (m > 0, m < n_mem - 1)

    def only(condition, action):
        pl.when(condition)(action)

    def z_peer(d):
        return my * NZ + lax.rem(mz + d, NZ)

    def y_peer(d):
        return lax.rem(my + d, n_y) * NZ + mz

    def wait_bytes(ref, sem):
        pltpu.make_async_copy(ref, ref, sem).wait()

    parts = 3
    share = own_x // parts

    def load_rhs(piece):
        rows = pl.ds(piece * share, share)
        return pltpu.make_async_copy(
            rhs_hbm.at[rows], res.at[0, rows, pl.ds(8, own_y), :], rhs_sem.at[piece]
        )

    load_inv = pltpu.make_async_copy(linv_hbm.at[pl.ds(edge, mid), :], lbuf, in_sem.at[1])
    load_cond = pltpu.make_async_copy(cond_hbm, cond, in_sem.at[2])
    load_basis = pltpu.make_async_copy(basis_hbm, basis_t, in_sem.at[3])
    load_basis.start()
    for piece in range(parts):
        load_rhs(piece).start()
    load_cond.start()

    barrier = pltpu.get_barrier_semaphore()

    def greet_grp(d, carry):
        pl.semaphore_signal(
            barrier, inc=1, device_id={"grp": lax.rem(g + d, n_grp)}, device_id_type=MESH
        )
        return carry

    lax.fori_loop(1, n_grp, greet_grp, 0)
    greets = n_grp - 1
    for peer in [z_peer(d) for d in range(1, NZ)] + [y_peer(d) for d in range(1, n_y)] + [m_up, m_dn]:
        pl.semaphore_signal(barrier, inc=1, device_id={"mem": peer}, device_id_type=MESH)
        greets += 1
    for g_side in (g_dn, g_up):
        for m_side in (m_dn, m_up):
            pl.semaphore_signal(
                barrier, inc=1, device_id={"grp": g_side, "mem": m_side}, device_id_type=MESH
            )
            greets += 1

    def wide_basis(i):
        return split(jnp.concatenate([basis_t[2 * i], basis_t[2 * i + 1]], axis=1))

    load_basis.wait()
    for i in range(own_x // 2):
        bres[i] = jnp.concatenate(wide_basis(i), axis=0)

    def prepare_basis():
        for i in range(own_x // 2):
            hi, lo = (v.astype(F32) for v in wide_basis(i))
            tall = jnp.transpose(jnp.concatenate([hi, lo, hi], axis=0))
            bcor[i] = tall.astype(BF16)
            for j in range(2):
                x = 2 * i + j
                bedge[pl.ds(x, 1), :] = tall[j * own_y : j * own_y + 1]
                bedge[pl.ds(own_x + x, 1), :] = tall[(j + 1) * own_y - 1 : (j + 1) * own_y]
        bcor_out[...] = bcor[...]
        brim[...] = jnp.transpose(bedge[...])[: 2 * modes].astype(BF16)

    own_rows = pl.ds(pl.multiple_of(m * modes, modes), modes)

    def restrict_rows(basis, rows):
        hi, lo = split(rows)
        both = dot(basis, hi)
        return both[:modes] + both[modes:] + dot(basis[:modes], lo)

    def restrict(it, first, last, total):
        for i in range(first, last):
            pair = res[it, pl.ds(2 * i, 2), pl.ds(8, own_y), :].reshape(2 * own_y, columns)
            total = total + restrict_rows(bres[i], pair)
        return total

    def put_restricted(it, total):
        for c in range(chunks):
            rblk[it, c, own_rows, :] = total[:, c * LANES : (c + 1) * LANES]

    def restrict_rhs():
        total = jnp.zeros((modes, columns), F32)
        for piece in range(parts):
            load_rhs(piece).wait()
            if piece == parts - 1:
                load_inv.start()
            total = restrict(0, piece * share // 2, (piece + 1) * share // 2, total)
        put_restricted(0, total)

    low_half = lax.broadcasted_iota(jnp.int32, (own_x // 2, 8, columns), 1) < OV

    def flip(v):
        return pltpu.roll(v, OV, 1)

    def pack_y(it):
        left = res[it, :, pl.ds(8, 8), :].reshape(own_x // 2, 2, 8, columns)
        right = res[it, :, pl.ds(own_y, 8), :].reshape(own_x // 2, 2, 8, columns)
        lo_side = jnp.where(low_half, left[:, 0], flip(left[:, 1]))
        hi_side = jnp.where(low_half, flip(right[:, 0]), right[:, 1])
        ysend[it, 0] = lo_side.reshape(own_x * OV, columns).astype(BF16)
        ysend[it, 1] = hi_side.reshape(own_x * OV, columns).astype(BF16)

    def y_copy(it, side):
        return pltpu.make_async_remote_copy(
            src_ref=ysend.at[it, side],
            dst_ref=wmar.at[it, y_rows(1 - side), :],
            send_sem=yh_send.at[side],
            recv_sem=yh_recv.at[it, 1 - side],
            device_id={"mem": m_dn if side == 0 else m_up},
            device_id_type=MESH,
        )

    def finish_y(it):
        for side in range(2):
            only(has_y[side], lambda side=side: y_copy(it, 1 - side).wait_recv())

            @pl.when(jnp.logical_not(has_y[side]))
            def _(side=side):
                wmar[it, y_rows(side), :] = jnp.zeros((y_margin, columns), BF16)

    def assemble(it):
        def row(x, carry):
            win[pl.ds(pl.multiple_of(x * span_y, span_y), span_y), :] = res[
                it, x, pl.ds(8 - OV, span_y), :
            ].astype(BF16)
            return carry

        lax.fori_loop(0, own_x, row, 0, unroll=4)

    def pack_x(it):
        for side, first in ((0, 0), (1, own_x - OV)):
            rows = res[it, pl.ds(first, OV), pl.ds(8, own_y), :]
            xsend[it, side] = rows.reshape(OV * own_y, columns).astype(BF16)

    def x_copy(it, side):
        return pltpu.make_async_remote_copy(
            src_ref=xsend.at[it, side],
            dst_ref=wmar.at[it, x_rows(1 - side), :],
            send_sem=xh_send.at[side],
            recv_sem=xh_recv.at[it, 1 - side],
            device_id={"grp": g_dn if side == 0 else g_up},
            device_id_type=MESH,
        )

    def corner_copy(it, side, y_side):
        first = 0 if side == 0 else (own_x - OV) * OV
        lands = (1 - side) * edge + OV * own_y + (1 - y_side) * OV * OV
        return pltpu.make_async_remote_copy(
            src_ref=ysend.at[it, y_side, pl.ds(first, OV * OV), :],
            dst_ref=wmar.at[it, pl.ds(lands, OV * OV), :],
            send_sem=co_send.at[side, y_side],
            recv_sem=co_recv.at[it, 1 - side, 1 - y_side],
            device_id={
                "grp": g_dn if side == 0 else g_up,
                "mem": m_dn if y_side == 0 else m_up,
            },
            device_id_type=MESH,
        )

    def corner_start(it):
        for side in range(2):
            for y_side in range(2):
                only(has_x[side] & has_y[y_side], corner_copy(it, side, y_side).start)

    def finish_x(it):
        for side in range(2):
            only(has_x[side], lambda side=side: x_copy(it, 1 - side).wait_recv())

            @pl.when(jnp.logical_not(has_x[side]))
            def _(side=side):
                wmar[it, x_rows(side), :] = jnp.zeros((OV * own_y, columns), BF16)

            for y_side in range(2):
                both = has_x[side] & has_y[y_side]
                only(both, lambda side=side, y_side=y_side: corner_copy(it, 1 - side, 1 - y_side).wait_recv())

                @pl.when(jnp.logical_not(both))
                def _(side=side, y_side=y_side):
                    lands = side * edge + OV * own_y + y_side * OV * OV
                    wmar[it, pl.ds(lands, OV * OV), :] = jnp.zeros((OV * OV, columns), BF16)

    chunk = OV * span_y

    def selector(shape, column_of):
        out = lax.broadcasted_iota(jnp.int32, shape, 1)
        into = lax.broadcasted_iota(jnp.int32, shape, 0)
        return jnp.where(into == column_of(out), 1.0, 0.0).astype(BF16)

    def x_column(n):
        row = sum((n >= own_y * k).astype(jnp.int32) for k in range(1, OV))
        corner = n - OV * own_y
        far = (corner >= OV * OV).astype(jnp.int32)
        corner = corner - far * OV * OV
        inside = row * (span_y - own_y) + n + OV
        outside = (corner // OV) * span_y + corner % OV + far * (span_y - OV)
        return jnp.where(n < OV * own_y, inside, outside)

    def y_column(n):
        far = (n >= y_margin).astype(jnp.int32)
        n = n - far * y_margin
        return (n // OV) * span_y + n % OV + far * (span_y - OV)

    def select_x():
        pick = selector((edge, edge), x_column)

        def step(i, carry):
            rows = pl.ds(pl.multiple_of(i * chunk, chunk), chunk)
            for side, first in ((0, 0), (1, edge + mid)):
                got = dot(lbuf[rows, pl.ds(first, edge)], pick)
                lmar[rows, pl.ds(side * edge, edge)] = got.astype(BF16)
            return carry

        lax.fori_loop(0, mid // chunk, step, 0)

    def select_y(first, last):
        if first == 0:
            ysel[...] = selector((mid, 2 * y_margin), y_column)

        def step(i, carry):
            rows = pl.ds(pl.multiple_of(i * chunk, chunk), chunk)
            got = dot(lbuf[rows, pl.ds(edge, mid)], ysel[...])
            lmar[rows, pl.ds(2 * edge, 2 * y_margin)] = got.astype(BF16)
            return carry

        lax.fori_loop(first, last, step, 0)

    def fine_inner(first, last):
        def step(i, carry):
            rows = pl.ds(pl.multiple_of(i * chunk, chunk), chunk)
            got = dot(lbuf[rows, pl.ds(edge, mid)], win[...])
            fine[pl.ds(i * OV, OV)] = got.reshape(OV, span_y, columns)
            return carry

        lax.fori_loop(first, last, step, 0)

    def fine_outer(it):
        def step(i, carry):
            rows = pl.ds(pl.multiple_of(i * chunk, chunk), chunk)
            got = dot(lmar[rows, :], wmar[it])
            fine[pl.ds(i * OV, OV)] += got.reshape(OV, span_y, columns)
            return carry

        lax.fori_loop(0, own_x // OV, step, 0)

    def z_copy(it, c, d):
        return pltpu.make_async_remote_copy(
            src_ref=rblk.at[it, c, own_rows, :], dst_ref=rblk.at[it, c, own_rows, :],
            send_sem=az_send, recv_sem=az_recv.at[it, c, d - 1],
            device_id={"mem": z_peer(d)}, device_id_type=MESH,
        )

    def y_forward(it, c, d, src_d):
        block = my * NZ + lax.rem(mz + NZ - src_d, NZ)
        rows = pl.ds(pl.multiple_of(block * modes, modes), modes)
        return pltpu.make_async_remote_copy(
            src_ref=rblk.at[it, c, rows, :], dst_ref=rblk.at[it, c, rows, :],
            send_sem=ay_send, recv_sem=ay_recv.at[it, c],
            device_id={"mem": y_peer(d)}, device_id_type=MESH,
        )

    def gather_start(it, c):
        for d in (2, 1, 3):
            z_copy(it, c, d).start()
        for d in range(1, n_y):
            y_forward(it, c, d, 0).start()

    def gather_forward(it, c, sources):
        for src_d in sources:
            z_copy(it, c, src_d).wait_recv()
            for d in range(1, n_y):
                y_forward(it, c, d, src_d).start()

    def gather_finish(it, c):
        wait_bytes(rblk.at[it, c, pl.ds(0, (n_y - 1) * NZ * modes), :], ay_recv.at[it, c])

    def c_copy(d):
        dest = lax.rem(g + d, n_grp)
        return pltpu.make_async_remote_copy(
            src_ref=cinv_hbm.at[:, pl.ds(pl.multiple_of(dest * n_mem * modes, n_mem * modes), n_mem * modes)],
            dst_ref=cblk.at[pl.ds(pl.multiple_of(g * modes, modes), modes), :],
            send_sem=c_send, recv_sem=c_recv,
            device_id={"grp": dest}, device_id_type=MESH,
        )

    c_local = pltpu.make_async_copy(
        cinv_hbm.at[:, pl.ds(pl.multiple_of(g * n_mem * modes, n_mem * modes), n_mem * modes)],
        cblk.at[pl.ds(pl.multiple_of(g * modes, modes), modes), :],
        cloc_sem,
    )

    def each_grp(action):
        def body(d, carry):
            action(d)
            return carry

        lax.fori_loop(1, n_grp, body, 0)

    def coarse_multiply(it, c):
        hi, lo = split(rblk[it, c])
        both = jnp.concatenate([hi, lo], axis=1)

        def step(i, carry):
            rows = pl.ds(pl.multiple_of(i * 128, 128), 128)
            two = dot(csplit[0, rows, :], both)
            got = two[:, :LANES] + (two[:, LANES:] + dot(csplit[1, rows, :], hi))
            part[it, c, pl.ds(i * 4, 4)] = got.reshape(4, 2, modes, LANES)
            return carry

        lax.fori_loop(0, n_grp * modes // 128, step, 0, unroll=True)

    def pair_copy(it, c):
        return pltpu.make_async_remote_copy(
            src_ref=part.at[it, c, :, 1 - core], dst_ref=pairbuf.at[it, c],
            send_sem=pr_send.at[c], recv_sem=pr_recv.at[it, c],
            device_id={"grp": 2 * pair + 1 - core}, device_id_type=MESH,
        )

    def rs_copy(it, c, d):
        dest = lax.rem(pair + d, n_pair)
        return pltpu.make_async_remote_copy(
            src_ref=sumbuf.at[it, c, dest], dst_ref=qbuf.at[it, c, d],
            send_sem=rs_send, recv_sem=rs_recv.at[it, c],
            device_id={"grp": 2 * dest + core}, device_id_type=MESH,
        )

    def pair_step(it, c):
        pair_copy(it, c).wait_recv()
        sumbuf[it, c] = part[it, c, :, core] + pairbuf[it, c]
        for d in range(1, n_pair):
            rs_copy(it, c, d).start()

    def lift(it):
        pieces = []
        for c in range(chunks):
            wait_bytes(qbuf.at[it, c, pl.ds(1, n_pair - 1)], rs_recv.at[it, c])
            total = sumbuf[it, c, pair]
            for d in range(1, n_pair):
                total = total + qbuf[it, c, d]
            pieces.append(total)
        hi, lo = split(jnp.concatenate(pieces, axis=1))
        return jnp.concatenate([hi.astype(F32), hi.astype(F32), lo.astype(F32)], axis=0).astype(BF16)

    def coarse_step(it, c):
        gather_finish(it, c)
        coarse_multiply(it, c)
        pair_copy(it, c).start()

    def drain(it):
        wait_bytes(rblk.at[it, :, pl.ds(0, (NZ - 1) * modes), :], az_send)
        wait_bytes(rblk.at[it, :, pl.ds(0, (n_y - 1) * NZ * modes), :], ay_send)
        for c in range(chunks):
            pair_copy(it, c).wait_send()
        for side in range(2):
            only(has_y[side], lambda side=side: y_copy(it, side).wait_send())
            only(has_x[side], lambda side=side: x_copy(it, side).wait_send())
            for y_side in range(2):
                only(
                    has_x[side] & has_y[y_side],
                    lambda side=side, y_side=y_side: corner_copy(it, side, y_side).wait_send(),
                )
        if it == 0:
            wait_bytes(cblk.at[pl.ds(0, (n_grp - 1) * modes), :], c_send)
            for slot in range(4):
                only((has_x + has_y)[slot ^ 1], lambda slot=slot: cond_copy(slot).wait_send())
            wait_bytes(sumbuf.at[0, :, pl.ds(1, n_pair - 1)], rs_send)

    def y_start(it):
        for side in range(2):
            only(has_y[side], y_copy(it, side).start)

    far_x = (g == n_grp // 2, g == n_grp // 2 - 1)

    def x_start(it, far):
        for side in range(2):
            there = far_x[side] if far else has_x[side] & jnp.logical_not(far_x[side])
            only(there, x_copy(it, side).start)

    def cond_copy(slot):
        if slot < 2:
            device = {"grp": g_up if slot == 0 else g_dn}
        else:
            device = {"mem": m_up if slot == 2 else m_dn}
        return pltpu.make_async_remote_copy(
            src_ref=cond, dst_ref=condrecv.at[slot],
            send_sem=cond_send.at[slot], recv_sem=cond_recv.at[slot],
            device_id=device, device_id_type=MESH,
        )

    def cond_start():
        for slot in range(4):
            only((has_x + has_y)[slot ^ 1], cond_copy(slot).start)

    def make_faces():
        for slot in range(4):
            only((has_x + has_y)[slot], lambda slot=slot: cond_copy(slot).wait_recv())
        shape = (own_y, own_y)
        eye = lax.broadcasted_iota(jnp.int32, shape, 0) == lax.broadcasted_iota(jnp.int32, shape, 1)
        lane = lax.broadcasted_iota(jnp.int32, (1, own_y), 1)

        def spread(row):
            full = jnp.where(eye, jnp.broadcast_to(row, shape), 0.0)
            return jnp.broadcast_to(jnp.sum(full, axis=1, keepdims=True), (own_y, 128))

        def pick(row, at):
            one = jnp.sum(jnp.where(lane == at, row, 0.0), axis=1, keepdims=True)
            return jnp.broadcast_to(one, (8, 128))

        def row_of(x, carry):
            cpad[x + 1, pl.ds(8, own_y), :] = spread(cond[pl.ds(x, 1), :])
            low = jnp.where(m == 0, 0.0, pick(condrecv[2, pl.ds(x, 1), :], own_y - 1))
            high = jnp.where(m == n_mem - 1, 0.0, pick(condrecv[3, pl.ds(x, 1), :], 0))
            cpad[x + 1, pl.ds(0, 8), :] = low
            cpad[x + 1, pl.ds(own_y + 8, 8), :] = high
            return carry

        lax.fori_loop(0, own_x, row_of, 0, unroll=4)
        first = jnp.where(g == 0, 0.0, condrecv[0, pl.ds(own_x - 1, 1), :])
        last = jnp.where(g == n_grp - 1, 0.0, condrecv[1, pl.ds(0, 1), :])
        cpad[0, pl.ds(8, own_y), :] = spread(first)
        cpad[own_x + 1, pl.ds(8, own_y), :] = spread(last)

        at_y = lax.broadcasted_iota(jnp.int32, (own_y + 8, 128), 0)
        inside = (at_y > 0) & (at_y < own_y)

        def face_x(x, carry):
            facex[x] = 0.5 * (cpad[x, pl.ds(8, own_y), :] + cpad[x + 1, pl.ds(8, own_y), :])
            return carry

        def face_y(x, carry):
            face = 0.5 * (cpad[x + 1, pl.ds(7, own_y + 8), :] + cpad[x + 1, pl.ds(8, own_y + 8), :])
            facey[x] = face
            inner_y[x] = jnp.where(inside, face, 0.0)
            return carry

        lax.fori_loop(0, own_x + 1, face_x, 0)
        lax.fori_loop(0, own_x, face_y, 0)

    def lanes(c):
        return pl.ds(c * LANES, LANES)

    def ex_copy(side, c):
        if side < 2:
            src = sol.at[1 if side == 0 else own_x, pl.ds(8, own_y), lanes(c)]
            dst = sol.at[own_x + 1 if side == 0 else 0, pl.ds(8, own_y), lanes(c)]
            device = {"grp": g_dn if side == 0 else g_up}
        else:
            src = esend.at[side - 2, c]
            dst = erecv.at[side - 2, c]
            device = {"mem": m_dn if side == 2 else m_up}
        return pltpu.make_async_remote_copy(
            src_ref=src, dst_ref=dst, send_sem=ex_send.at[side], recv_sem=ex_recv.at[side, c],
            device_id=device, device_id_type=MESH,
        )

    def sol_rows(i, lifted):
        co = dot(bcor[i], lifted)
        for j in range(2):
            value = fine[2 * i + j, pl.ds(OV, own_y), :] + co[j * own_y : (j + 1) * own_y]
            sol[2 * i + j + 1, pl.ds(8, own_y), :] = value

    def correct_edges(lifted):
        co = dot(bedge[...].astype(BF16), lifted)
        low = fine[:, OV, :] + co[:own_x]
        high = fine[:, OV + own_y - 1, :] + co[own_x:]
        for c in range(chunks):
            esend[0, c] = low[:, c * LANES : (c + 1) * LANES]
            esend[1, c] = high[:, c * LANES : (c + 1) * LANES]
        sol_rows(0, lifted)
        sol_rows(own_x // 2 - 1, lifted)

    def ex_start():
        for c in range(chunks):
            for side in (2, 3, 0, 1):
                only((has_x + has_y)[side], ex_copy(side, c).start)

    def correct_inner(lifted):
        def step(i, carry):
            sol_rows(i, lifted)
            return carry

        lax.fori_loop(1, own_x // 2 - 1, step, 0, unroll=True)

    def zero_margin():
        zero = jnp.zeros((8, columns), F32)
        for x in range(own_x):
            sol[x + 1, pl.ds(0, 8), :] = zero
            sol[x + 1, pl.ds(own_y + 8, 8), :] = zero
            for it in range(2):
                res[it, x, pl.ds(0, 8), :] = zero
                res[it, x, pl.ds(own_y + 8, 8), :] = zero

    def thrice(v):
        return jnp.concatenate([v] * (columns // 128), axis=1)

    def inner_residual():
        def row(x, first, last):
            c = sol[x + 1, pl.ds(8, own_y), :]
            total = thrice(inner_y[x, pl.ds(1, own_y), :]) * (c - sol[x + 1, pl.ds(9, own_y), :])
            total += thrice(inner_y[x, pl.ds(0, own_y), :]) * (c - sol[x + 1, pl.ds(7, own_y), :])
            if not last:
                total += thrice(facex[x + 1]) * (c - sol[x + 2, pl.ds(8, own_y), :])
            if not first:
                total += thrice(facex[x]) * (c - sol[x, pl.ds(8, own_y), :])
            res[1, x, pl.ds(8, own_y), :] = res[0, x, pl.ds(8, own_y), :] - total

        def step(x, carry):
            row(x, False, False)
            return carry

        row(0, True, False)
        lax.fori_loop(1, own_x - 1, step, 0, unroll=2)
        row(own_x - 1, False, True)

    def rim_changes(c):
        for side in range(4):
            only((has_x + has_y)[side ^ 1], lambda side=side: ex_copy(side, c).wait_recv())
        low_x = jnp.where(g == 0, 0.0, sol[0, pl.ds(8, own_y), lanes(c)])
        high_x = jnp.where(g == n_grp - 1, 0.0, sol[own_x + 1, pl.ds(8, own_y), lanes(c)])
        low_x = facex[0] * (sol[1, pl.ds(8, own_y), lanes(c)] - low_x)
        high_x = facex[own_x] * (sol[own_x, pl.ds(8, own_y), lanes(c)] - high_x)
        low_y = facey[:, 0, :] * (esend[0, c] - jnp.where(m == 0, 0.0, erecv[1, c]))
        high_y = facey[:, own_y, :] * (esend[1, c] - jnp.where(m == n_mem - 1, 0.0, erecv[0, c]))
        return low_x, high_x, low_y, high_y

    def restrict_rim(c, total, low_x, high_x, low_y, high_y):
        zero = jnp.zeros_like(low_x)
        total = total - restrict_rows(bres[0], jnp.concatenate([low_x, zero], axis=0))
        total = total - restrict_rows(bres[own_x // 2 - 1], jnp.concatenate([zero, high_x], axis=0))
        total = total - restrict_rows(brim[...], jnp.concatenate([low_y, high_y], axis=0))
        rblk[1, c, own_rows, :] = total

    def rim_step(c, total):
        rim = rim_changes(c)
        restrict_rim(c, total[:, c * LANES : (c + 1) * LANES], *rim)
        gather_start(1, c)
        return rim

    def outer_residual(c, low_x, high_x, low_y, high_y):
        res[1, 0, pl.ds(8, own_y), lanes(c)] -= low_x
        res[1, own_x - 1, pl.ds(8, own_y), lanes(c)] -= high_x
        res[1, :, 8, lanes(c)] -= low_y
        res[1, :, own_y + 7, lanes(c)] -= high_y

    def finish_base():
        def step(x, carry):
            base_out[x] = sol[x + 1, pl.ds(8, own_y), :] + fine[x, pl.ds(OV, own_y), :]
            return carry

        lax.fori_loop(0, own_x, step, 0, unroll=2)

    blocks = mid // chunk
    restrict_rhs()
    load_cond.wait()
    pl.semaphore_wait(barrier, greets)
    for c in range(chunks):
        gather_start(0, c)
    cond_start()
    each_grp(lambda d: c_copy(d).start())
    c_local.start()
    prepare_basis()
    zero_margin()
    pack_x(0)
    pack_y(0)
    assemble(0)
    load_inv.wait()
    select_x()
    fine_inner(0, 3)
    gather_forward(0, 0, (1, 3, 2))
    gather_forward(0, 1, (1, 3, 2))
    gather_forward(0, 2, (1, 3, 2))
    x_start(0, True)
    x_start(0, False)
    corner_start(0)
    fine_inner(3, 4)
    y_start(0)
    fine_inner(4, blocks)
    make_faces()
    wait_bytes(cblk.at[pl.ds(0, (n_grp - 1) * modes), :], c_recv)
    c_local.wait()
    csplit[0], csplit[1] = split(cblk[...])
    coarse_step(0, 0)
    coarse_step(0, 1)
    select_y(0, 1)
    pair_step(0, 0)
    coarse_step(0, 2)
    pair_step(0, 1)
    select_y(1, 2)
    pair_step(0, 2)
    select_y(2, blocks)
    finish_y(0)
    finish_x(0)
    fine_outer(0)
    lifted = lift(0)
    correct_edges(lifted)
    ex_start()
    correct_inner(lifted)
    inner_residual()

    inner = restrict(1, 0, own_x // 2, jnp.zeros((modes, columns), F32))
    drain(0)
    rim_0 = rim_step(0, inner)
    rim_1 = rim_step(1, inner)
    rim_2 = rim_step(2, inner)
    outer_residual(0, *rim_0)
    outer_residual(1, *rim_1)
    outer_residual(2, *rim_2)
    pack_x(1)
    x_start(1, True)
    x_start(1, False)
    pack_y(1)
    corner_start(1)
    assemble(1)
    gather_forward(1, 0, (1, 3, 2))
    gather_forward(1, 1, (1, 3, 2))
    gather_forward(1, 2, (1, 3, 2))
    fine_inner(0, 2)
    y_start(1)
    fine_inner(2, 4)
    coarse_step(1, 0)
    coarse_step(1, 1)
    pair_step(1, 0)
    coarse_step(1, 2)
    pair_step(1, 1)
    fine_inner(4, 5)
    pair_step(1, 2)
    fine_inner(5, blocks)
    finish_y(1)
    finish_x(1)
    fine_outer(1)
    finish_base()
    drain(1)
    lifted_out[...] = lift(1)

    for side in range(4):
        sent = sol.at[1, pl.ds(8, own_y), :] if side < 2 else esend.at[side - 2]
        only((has_x + has_y)[side], lambda side=side, sent=sent: wait_bytes(sent, ex_send.at[side]))
    wait_bytes(sumbuf.at[1, :, pl.ds(1, n_pair - 1)], rs_send)


def tail_kernel(base, lifted, bcor, out_hbm, outbuf, out_sem):
    pairs, own_y = base.shape[0] // 2, base.shape[1]
    per = 3

    def store(i):
        rows = pl.ds(2 * per * i, 2 * per)
        return pltpu.make_async_copy(outbuf.at[rows], out_hbm.at[rows], out_sem.at[i])

    for i in range(pairs // per):
        for k in range(per * i, per * i + per):
            co = dot(bcor[k], lifted[...])
            for j in range(2):
                outbuf[2 * k + j] = base[2 * k + j] + co[j * own_y : (j + 1) * own_y]
        store(i).start()
    for i in range(pairs // per):
        store(i).wait()


def on_device(rhs, conductivity, local_inverse, coarse_basis, coarse_inverse):
    own_x, own_y, columns = rhs.shape
    modes = coarse_basis.shape[2]
    n_grp, n_mem = lax.axis_size("grp"), lax.axis_size("mem")
    n_y = n_mem // NZ
    chunks = columns // LANES
    span_x, span_y = own_x + 2 * OV, own_y + 2 * OV
    basis_t = jnp.transpose(coarse_basis, (0, 2, 1))
    arrays = (rhs, conductivity, local_inverse, basis_t, coarse_inverse)
    hbm = pl.BlockSpec(memory_space=pltpu.HBM)
    vmem = pl.BlockSpec(memory_space=pltpu.VMEM)
    dma = pltpu.SemaphoreType.DMA
    scratch = [
        pltpu.VMEM((own_x, own_y), F32),
        pltpu.VMEM((own_x, modes, own_y), F32),
        pltpu.VMEM((own_x * span_y, span_x * span_y), BF16),
        pltpu.VMEM((2, own_x, own_y + 16, columns), F32),
        pltpu.VMEM((own_x * span_y, columns), BF16),
        pltpu.VMEM((2, 2 * OV * (span_y + own_x), columns), BF16),
        pltpu.VMEM((own_x * span_y, 2 * OV * (span_y + own_x)), BF16),
        pltpu.VMEM((own_x * span_y, 2 * OV * own_x), BF16),
        pltpu.VMEM((own_x, span_y, columns), F32),
        pltpu.VMEM((own_x + 2, own_y + 16, columns), F32),
        pltpu.VMEM((own_x + 2, own_y + 16, 128), F32),
        pltpu.VMEM((own_x + 1, own_y, 128), F32),
        pltpu.VMEM((own_x, own_y + 8, 128), F32),
        pltpu.VMEM((own_x, own_y + 8, 128), F32),
        pltpu.VMEM((own_x // 2, 2 * modes, 2 * own_y), BF16),
        pltpu.VMEM((own_x // 2, 2 * own_y, 3 * modes), BF16),
        pltpu.VMEM((2 * own_x, 3 * modes), F32),
        pltpu.VMEM((2 * modes, 2 * own_x), BF16),
        pltpu.VMEM((2, chunks, n_mem * modes, LANES), F32),
        pltpu.VMEM((n_grp * modes, n_mem * modes), F32),
        pltpu.VMEM((2, n_grp * modes, n_mem * modes), BF16),
        pltpu.VMEM((2, chunks, n_grp // 2, 2, modes, LANES), F32),
        pltpu.VMEM((2, chunks, n_grp // 2, modes, LANES), F32),
        pltpu.VMEM((2, chunks, n_grp // 2, modes, LANES), F32),
        pltpu.VMEM((2, chunks, n_grp // 2, modes, LANES), F32),
        pltpu.VMEM((2, 2, own_x * OV, columns), BF16),
        pltpu.VMEM((2, 2, OV * own_y, columns), BF16),
        pltpu.VMEM((2, chunks, own_x, LANES), F32),
        pltpu.VMEM((2, chunks, own_x, LANES), F32),
        pltpu.VMEM((4, own_x, own_y), F32),
        dma((4,)), dma((3,)), dma,
        dma, dma, dma((4,)), dma((4,)),
        dma, dma((2, chunks, NZ - 1)), dma, dma((2, chunks)),
        dma((chunks,)), dma((2, chunks)), dma, dma((2, chunks)),
        dma((2,)), dma((2, 2)), dma((2,)), dma((2, 2)), dma((2, 2)), dma((2, 2, 2)),
        dma((4,)), dma((4, chunks)),
    ]
    base, lifted, bcor = pl.pallas_call(
        functools.partial(kernel, n_grp, n_mem, own_x, own_y),
        out_shape=(
            jax.ShapeDtypeStruct(rhs.shape, F32),
            jax.ShapeDtypeStruct((3 * modes, columns), BF16),
            jax.ShapeDtypeStruct((own_x // 2, 2 * own_y, 3 * modes), BF16),
        ),
        in_specs=[hbm] * 5,
        out_specs=(vmem, vmem, vmem),
        scratch_shapes=scratch,
        compiler_params=pltpu.CompilerParams(
            collective_id=0, has_side_effects=True, vmem_limit_bytes=44 * 1024 * 1024
        ),
    )(*(pltpu.with_memory_space_constraint(v, pltpu.HBM) for v in arrays))
    return pl.pallas_call(
        tail_kernel,
        out_shape=jax.ShapeDtypeStruct(rhs.shape, F32),
        in_specs=[vmem, vmem, vmem],
        out_specs=hbm,
        scratch_shapes=[pltpu.VMEM(rhs.shape, F32), dma((own_x // 6,))],
        compiler_params=pltpu.CompilerParams(vmem_limit_bytes=16 * 1024 * 1024),
    )(base, lifted, bcor)


def solution(mesh):
    placed = (
        P("grp", "mem", None),
        P("grp", "mem"),
        P(("grp", "mem"), None),
        P("grp", "mem", None),
        P(("grp", "mem"), None),
    )
    return jax.shard_map(
        on_device, mesh=mesh, in_specs=placed, out_specs=P("grp", "mem", None), check_vma=False
    )
```

```python
import functools
import jax
import jax.numpy as jnp
from jax import lax
from jax.experimental import pallas as pl
from jax.experimental.pallas import tpu as pltpu
from jax.sharding import PartitionSpec as P

OV = 4
LANES = 128
NZ = 4
MESH = pl.DeviceIdType.MESH
F32 = jnp.float32
BF16 = jnp.bfloat16


def split(v):
    hi = v.astype(BF16)
    lo = (v - hi.astype(F32)).astype(BF16)
    return hi, lo


def dot(a, b):
    return jnp.dot(a, b, preferred_element_type=F32)


def kernel(
    n_grp, n_mem, own_x, own_y,
    rhs_hbm, cond_hbm, linv_hbm, basis_hbm, cinv_hbm,
    base_out, lifted_out, bcor_out,
    cond, basis_t, lbuf, res, win, wmar, lmar, ysel, fine, sol, cpad, facex, facey, inner_y,
    bres, bcor, bedge, brim, rblk, cblk, csplit, part, pairbuf, sumbuf, qbuf,
    ysend, xsend, esend, erecv, condrecv,
    in_sem, rhs_sem, cloc_sem,
    c_send, c_recv, cond_send, cond_recv,
    az_send, az_recv, ay_send, ay_recv, pr_send, pr_recv, rs_send, rs_recv,
    yh_send, yh_recv, xh_send, xh_recv, co_send, co_recv, ex_send, ex_recv,
):
    g = lax.axis_index("grp")
    m = lax.axis_index("mem")
    n_y = n_mem // NZ
    my = m // NZ
    mz = lax.rem(m, NZ)
    n_pair = n_grp // 2
    pair = g // 2
    core = lax.rem(g, 2)
    span_y = own_y + 2 * OV
    columns = rhs_hbm.shape[2]
    modes = basis_hbm.shape[1]
    chunks = columns // LANES
    edge = OV * span_y
    y_margin = own_x * OV

    def y_rows(side):
        return pl.ds(2 * edge + side * y_margin, y_margin)

    def x_rows(side):
        return pl.ds(side * edge, OV * own_y)

    mid = own_x * span_y
    g_up = lax.rem(g + 1, n_grp)
    g_dn = lax.rem(g + n_grp - 1, n_grp)
    m_up = lax.rem(m + 1, n_mem)
    m_dn = lax.rem(m + n_mem - 1, n_mem)

    has_x = (g > 0, g < n_grp - 1)
    has_y = (m > 0, m < n_mem - 1)

    def only(condition, action):
        pl.when(condition)(action)

    def z_peer(d):
        return my * NZ + lax.rem(mz + d, NZ)

    def y_peer(d):
        return lax.rem(my + d, n_y) * NZ + mz

    def wait_bytes(ref, sem):
        pltpu.make_async_copy(ref, ref, sem).wait()

    parts = 3
    share = own_x // parts

    def load_rhs(piece):
        rows = pl.ds(piece * share, share)
        return pltpu.make_async_copy(
            rhs_hbm.at[rows], res.at[0, rows, pl.ds(8, own_y), :], rhs_sem.at[piece]
        )

    load_inv = pltpu.make_async_copy(linv_hbm.at[pl.ds(edge, mid), :], lbuf, in_sem.at[1])
    load_cond = pltpu.make_async_copy(cond_hbm, cond, in_sem.at[2])
    load_basis = pltpu.make_async_copy(basis_hbm, basis_t, in_sem.at[3])
    load_basis.start()
    for piece in range(parts):
        load_rhs(piece).start()
    load_cond.start()

    barrier = pltpu.get_barrier_semaphore()

    def greet_grp(d, carry):
        pl.semaphore_signal(
            barrier, inc=1, device_id={"grp": lax.rem(g + d, n_grp)}, device_id_type=MESH
        )
        return carry

    lax.fori_loop(1, n_grp, greet_grp, 0)
    greets = n_grp - 1
    for peer in [z_peer(d) for d in range(1, NZ)] + [y_peer(d) for d in range(1, n_y)] + [m_up, m_dn]:
        pl.semaphore_signal(barrier, inc=1, device_id={"mem": peer}, device_id_type=MESH)
        greets += 1
    for g_side in (g_dn, g_up):
        for m_side in (m_dn, m_up):
            pl.semaphore_signal(
                barrier, inc=1, device_id={"grp": g_side, "mem": m_side}, device_id_type=MESH
            )
            greets += 1

    def wide_basis(i):
        return split(jnp.concatenate([basis_t[2 * i], basis_t[2 * i + 1]], axis=1))

    load_basis.wait()
    for i in range(own_x // 2):
        bres[i] = jnp.concatenate(wide_basis(i), axis=0)

    def prepare_basis():
        for i in range(own_x // 2):
            hi, lo = (v.astype(F32) for v in wide_basis(i))
            tall = jnp.transpose(jnp.concatenate([hi, lo, hi], axis=0))
            bcor[i] = tall.astype(BF16)
            for j in range(2):
                x = 2 * i + j
                bedge[pl.ds(x, 1), :] = tall[j * own_y : j * own_y + 1]
                bedge[pl.ds(own_x + x, 1), :] = tall[(j + 1) * own_y - 1 : (j + 1) * own_y]
        bcor_out[...] = bcor[...]
        brim[...] = jnp.transpose(bedge[...])[: 2 * modes].astype(BF16)

    own_rows = pl.ds(pl.multiple_of(m * modes, modes), modes)

    def restrict_rows(basis, rows):
        hi, lo = split(rows)
        both = dot(basis, hi)
        return both[:modes] + both[modes:] + dot(basis[:modes], lo)

    def restrict(it, first, last, total):
        for i in range(first, last):
            pair = res[it, pl.ds(2 * i, 2), pl.ds(8, own_y), :].reshape(2 * own_y, columns)
            total = total + restrict_rows(bres[i], pair)
        return total

    def put_restricted(it, total):
        for c in range(chunks):
            rblk[it, c, own_rows, :] = total[:, c * LANES : (c + 1) * LANES]

    def restrict_rhs():
        total = jnp.zeros((modes, columns), F32)
        for piece in range(parts):
            load_rhs(piece).wait()
            if piece == parts - 1:
                load_inv.start()
            total = restrict(0, piece * share // 2, (piece + 1) * share // 2, total)
        put_restricted(0, total)

    low_half = lax.broadcasted_iota(jnp.int32, (own_x // 2, 8, columns), 1) < OV

    def flip(v):
        return pltpu.roll(v, OV, 1)

    def pack_y(it):
        left = res[it, :, pl.ds(8, 8), :].reshape(own_x // 2, 2, 8, columns)
        right = res[it, :, pl.ds(own_y, 8), :].reshape(own_x // 2, 2, 8, columns)
        lo_side = jnp.where(low_half, left[:, 0], flip(left[:, 1]))
        hi_side = jnp.where(low_half, flip(right[:, 0]), right[:, 1])
        ysend[it, 0] = lo_side.reshape(own_x * OV, columns).astype(BF16)
        ysend[it, 1] = hi_side.reshape(own_x * OV, columns).astype(BF16)

    def y_copy(it, side):
        return pltpu.make_async_remote_copy(
            src_ref=ysend.at[it, side],
            dst_ref=wmar.at[it, y_rows(1 - side), :],
            send_sem=yh_send.at[side],
            recv_sem=yh_recv.at[it, 1 - side],
            device_id={"mem": m_dn if side == 0 else m_up},
            device_id_type=MESH,
        )

    def finish_y(it):
        for side in range(2):
            only(has_y[side], lambda side=side: y_copy(it, 1 - side).wait_recv())

            @pl.when(jnp.logical_not(has_y[side]))
            def _(side=side):
                wmar[it, y_rows(side), :] = jnp.zeros((y_margin, columns), BF16)

    def assemble(it):
        def row(x, carry):
            win[pl.ds(pl.multiple_of(x * span_y, span_y), span_y), :] = res[
                it, x, pl.ds(8 - OV, span_y), :
            ].astype(BF16)
            return carry

        lax.fori_loop(0, own_x, row, 0, unroll=4)

    def pack_x(it):
        for side, first in ((0, 0), (1, own_x - OV)):
            rows = res[it, pl.ds(first, OV), pl.ds(8, own_y), :]
            xsend[it, side] = rows.reshape(OV * own_y, columns).astype(BF16)

    def x_copy(it, side):
        return pltpu.make_async_remote_copy(
            src_ref=xsend.at[it, side],
            dst_ref=wmar.at[it, x_rows(1 - side), :],
            send_sem=xh_send.at[side],
            recv_sem=xh_recv.at[it, 1 - side],
            device_id={"grp": g_dn if side == 0 else g_up},
            device_id_type=MESH,
        )

    def corner_copy(it, side, y_side):
        first = 0 if side == 0 else (own_x - OV) * OV
        lands = (1 - side) * edge + OV * own_y + (1 - y_side) * OV * OV
        return pltpu.make_async_remote_copy(
            src_ref=ysend.at[it, y_side, pl.ds(first, OV * OV), :],
            dst_ref=wmar.at[it, pl.ds(lands, OV * OV), :],
            send_sem=co_send.at[side, y_side],
            recv_sem=co_recv.at[it, 1 - side, 1 - y_side],
            device_id={
                "grp": g_dn if side == 0 else g_up,
                "mem": m_dn if y_side == 0 else m_up,
            },
            device_id_type=MESH,
        )

    def corner_start(it):
        for side in range(2):
            for y_side in range(2):
                only(has_x[side] & has_y[y_side], corner_copy(it, side, y_side).start)

    def finish_x(it):
        for side in range(2):
            only(has_x[side], lambda side=side: x_copy(it, 1 - side).wait_recv())

            @pl.when(jnp.logical_not(has_x[side]))
            def _(side=side):
                wmar[it, x_rows(side), :] = jnp.zeros((OV * own_y, columns), BF16)

            for y_side in range(2):
                both = has_x[side] & has_y[y_side]
                only(both, lambda side=side, y_side=y_side: corner_copy(it, 1 - side, 1 - y_side).wait_recv())

                @pl.when(jnp.logical_not(both))
                def _(side=side, y_side=y_side):
                    lands = side * edge + OV * own_y + y_side * OV * OV
                    wmar[it, pl.ds(lands, OV * OV), :] = jnp.zeros((OV * OV, columns), BF16)

    chunk = OV * span_y

    def selector(shape, column_of):
        out = lax.broadcasted_iota(jnp.int32, shape, 1)
        into = lax.broadcasted_iota(jnp.int32, shape, 0)
        return jnp.where(into == column_of(out), 1.0, 0.0).astype(BF16)

    def x_column(n):
        row = sum((n >= own_y * k).astype(jnp.int32) for k in range(1, OV))
        corner = n - OV * own_y
        far = (corner >= OV * OV).astype(jnp.int32)
        corner = corner - far * OV * OV
        inside = row * (span_y - own_y) + n + OV
        outside = (corner // OV) * span_y + corner % OV + far * (span_y - OV)
        return jnp.where(n < OV * own_y, inside, outside)

    def y_column(n):
        far = (n >= y_margin).astype(jnp.int32)
        n = n - far * y_margin
        return (n // OV) * span_y + n % OV + far * (span_y - OV)

    def select_x():
        pick = selector((edge, edge), x_column)

        def step(i, carry):
            rows = pl.ds(pl.multiple_of(i * chunk, chunk), chunk)
            for side, first in ((0, 0), (1, edge + mid)):
                got = dot(lbuf[rows, pl.ds(first, edge)], pick)
                lmar[rows, pl.ds(side * edge, edge)] = got.astype(BF16)
            return carry

        lax.fori_loop(0, mid // chunk, step, 0)

    def select_y(first, last):
        if first == 0:
            ysel[...] = selector((mid, 2 * y_margin), y_column)

        def step(i, carry):
            rows = pl.ds(pl.multiple_of(i * chunk, chunk), chunk)
            got = dot(lbuf[rows, pl.ds(edge, mid)], ysel[...])
            lmar[rows, pl.ds(2 * edge, 2 * y_margin)] = got.astype(BF16)
            return carry

        lax.fori_loop(first, last, step, 0)

    def fine_inner(first, last):
        def step(i, carry):
            rows = pl.ds(pl.multiple_of(i * chunk, chunk), chunk)
            got = dot(lbuf[rows, pl.ds(edge, mid)], win[...])
            fine[pl.ds(i * OV, OV)] = got.reshape(OV, span_y, columns)
            return carry

        lax.fori_loop(first, last, step, 0)

    def fine_outer(it):
        def step(i, carry):
            rows = pl.ds(pl.multiple_of(i * chunk, chunk), chunk)
            got = dot(lmar[rows, :], wmar[it])
            fine[pl.ds(i * OV, OV)] += got.reshape(OV, span_y, columns)
            return carry

        lax.fori_loop(0, own_x // OV, step, 0)

    def z_copy(it, c, d):
        return pltpu.make_async_remote_copy(
            src_ref=rblk.at[it, c, own_rows, :], dst_ref=rblk.at[it, c, own_rows, :],
            send_sem=az_send, recv_sem=az_recv.at[it, c, d - 1],
            device_id={"mem": z_peer(d)}, device_id_type=MESH,
        )

    def y_forward(it, c, d, src_d):
        block = my * NZ + lax.rem(mz + NZ - src_d, NZ)
        rows = pl.ds(pl.multiple_of(block * modes, modes), modes)
        return pltpu.make_async_remote_copy(
            src_ref=rblk.at[it, c, rows, :], dst_ref=rblk.at[it, c, rows, :],
            send_sem=ay_send, recv_sem=ay_recv.at[it, c],
            device_id={"mem": y_peer(d)}, device_id_type=MESH,
        )

    def gather_start(it, c):
        for d in (2, 1, 3):
            z_copy(it, c, d).start()
        for d in range(1, n_y):
            y_forward(it, c, d, 0).start()

    def gather_forward(it, c, sources):
        for src_d in sources:
            z_copy(it, c, src_d).wait_recv()
            for d in range(1, n_y):
                y_forward(it, c, d, src_d).start()

    def gather_finish(it, c):
        wait_bytes(rblk.at[it, c, pl.ds(0, (n_y - 1) * NZ * modes), :], ay_recv.at[it, c])

    def c_copy(d):
        dest = lax.rem(g + d, n_grp)
        return pltpu.make_async_remote_copy(
            src_ref=cinv_hbm.at[:, pl.ds(pl.multiple_of(dest * n_mem * modes, n_mem * modes), n_mem * modes)],
            dst_ref=cblk.at[pl.ds(pl.multiple_of(g * modes, modes), modes), :],
            send_sem=c_send, recv_sem=c_recv,
            device_id={"grp": dest}, device_id_type=MESH,
        )

    c_local = pltpu.make_async_copy(
        cinv_hbm.at[:, pl.ds(pl.multiple_of(g * n_mem * modes, n_mem * modes), n_mem * modes)],
        cblk.at[pl.ds(pl.multiple_of(g * modes, modes), modes), :],
        cloc_sem,
    )

    def each_grp(action):
        def body(d, carry):
            action(d)
            return carry

        lax.fori_loop(1, n_grp, body, 0)

    def coarse_multiply(it, c):
        hi, lo = split(rblk[it, c])
        both = jnp.concatenate([hi, lo], axis=1)

        def step(i, carry):
            rows = pl.ds(pl.multiple_of(i * 128, 128), 128)
            two = dot(csplit[0, rows, :], both)
            got = two[:, :LANES] + (two[:, LANES:] + dot(csplit[1, rows, :], hi))
            part[it, c, pl.ds(i * 4, 4)] = got.reshape(4, 2, modes, LANES)
            return carry

        lax.fori_loop(0, n_grp * modes // 128, step, 0, unroll=True)

    def pair_copy(it, c):
        return pltpu.make_async_remote_copy(
            src_ref=part.at[it, c, :, 1 - core], dst_ref=pairbuf.at[it, c],
            send_sem=pr_send.at[c], recv_sem=pr_recv.at[it, c],
            device_id={"grp": 2 * pair + 1 - core}, device_id_type=MESH,
        )

    def rs_copy(it, c, d):
        dest = lax.rem(pair + d, n_pair)
        return pltpu.make_async_remote_copy(
            src_ref=sumbuf.at[it, c, dest], dst_ref=qbuf.at[it, c, d],
            send_sem=rs_send, recv_sem=rs_recv.at[it, c],
            device_id={"grp": 2 * dest + core}, device_id_type=MESH,
        )

    def pair_step(it, c):
        pair_copy(it, c).wait_recv()
        sumbuf[it, c] = part[it, c, :, core] + pairbuf[it, c]
        for d in range(1, n_pair):
            rs_copy(it, c, d).start()

    def lift(it):
        pieces = []
        for c in range(chunks):
            wait_bytes(qbuf.at[it, c, pl.ds(1, n_pair - 1)], rs_recv.at[it, c])
            total = sumbuf[it, c, pair]
            for d in range(1, n_pair):
                total = total + qbuf[it, c, d]
            pieces.append(total)
        hi, lo = split(jnp.concatenate(pieces, axis=1))
        return jnp.concatenate([hi.astype(F32), hi.astype(F32), lo.astype(F32)], axis=0).astype(BF16)

    def coarse_step(it, c):
        gather_finish(it, c)
        coarse_multiply(it, c)
        pair_copy(it, c).start()

    def drain(it):
        wait_bytes(rblk.at[it, :, pl.ds(0, (NZ - 1) * modes), :], az_send)
        wait_bytes(rblk.at[it, :, pl.ds(0, (n_y - 1) * NZ * modes), :], ay_send)
        for c in range(chunks):
            pair_copy(it, c).wait_send()
        for side in range(2):
            only(has_y[side], lambda side=side: y_copy(it, side).wait_send())
            only(has_x[side], lambda side=side: x_copy(it, side).wait_send())
            for y_side in range(2):
                only(
                    has_x[side] & has_y[y_side],
                    lambda side=side, y_side=y_side: corner_copy(it, side, y_side).wait_send(),
                )
        if it == 0:
            wait_bytes(cblk.at[pl.ds(0, (n_grp - 1) * modes), :], c_send)
            for slot in range(4):
                only((has_x + has_y)[slot ^ 1], lambda slot=slot: cond_copy(slot).wait_send())
            wait_bytes(sumbuf.at[0, :, pl.ds(1, n_pair - 1)], rs_send)

    def y_start(it):
        for side in range(2):
            only(has_y[side], y_copy(it, side).start)

    far_x = (g == n_grp // 2, g == n_grp // 2 - 1)

    def x_start(it, far):
        for side in range(2):
            there = far_x[side] if far else has_x[side] & jnp.logical_not(far_x[side])
            only(there, x_copy(it, side).start)

    def cond_copy(slot):
        if slot < 2:
            device = {"grp": g_up if slot == 0 else g_dn}
        else:
            device = {"mem": m_up if slot == 2 else m_dn}
        return pltpu.make_async_remote_copy(
            src_ref=cond, dst_ref=condrecv.at[slot],
            send_sem=cond_send.at[slot], recv_sem=cond_recv.at[slot],
            device_id=device, device_id_type=MESH,
        )

    def cond_start():
        for slot in range(4):
            only((has_x + has_y)[slot ^ 1], cond_copy(slot).start)

    def make_faces():
        for slot in range(4):
            only((has_x + has_y)[slot], lambda slot=slot: cond_copy(slot).wait_recv())
        shape = (own_y, own_y)
        eye = lax.broadcasted_iota(jnp.int32, shape, 0) == lax.broadcasted_iota(jnp.int32, shape, 1)
        lane = lax.broadcasted_iota(jnp.int32, (1, own_y), 1)

        def spread(row):
            full = jnp.where(eye, jnp.broadcast_to(row, shape), 0.0)
            return jnp.broadcast_to(jnp.sum(full, axis=1, keepdims=True), (own_y, 128))

        def pick(row, at):
            one = jnp.sum(jnp.where(lane == at, row, 0.0), axis=1, keepdims=True)
            return jnp.broadcast_to(one, (8, 128))

        def row_of(x, carry):
            cpad[x + 1, pl.ds(8, own_y), :] = spread(cond[pl.ds(x, 1), :])
            low = jnp.where(m == 0, 0.0, pick(condrecv[2, pl.ds(x, 1), :], own_y - 1))
            high = jnp.where(m == n_mem - 1, 0.0, pick(condrecv[3, pl.ds(x, 1), :], 0))
            cpad[x + 1, pl.ds(0, 8), :] = low
            cpad[x + 1, pl.ds(own_y + 8, 8), :] = high
            return carry

        lax.fori_loop(0, own_x, row_of, 0, unroll=4)
        first = jnp.where(g == 0, 0.0, condrecv[0, pl.ds(own_x - 1, 1), :])
        last = jnp.where(g == n_grp - 1, 0.0, condrecv[1, pl.ds(0, 1), :])
        cpad[0, pl.ds(8, own_y), :] = spread(first)
        cpad[own_x + 1, pl.ds(8, own_y), :] = spread(last)

        at_y = lax.broadcasted_iota(jnp.int32, (own_y + 8, 128), 0)
        inside = (at_y > 0) & (at_y < own_y)

        def face_x(x, carry):
            facex[x] = 0.5 * (cpad[x, pl.ds(8, own_y), :] + cpad[x + 1, pl.ds(8, own_y), :])
            return carry

        def face_y(x, carry):
            face = 0.5 * (cpad[x + 1, pl.ds(7, own_y + 8), :] + cpad[x + 1, pl.ds(8, own_y + 8), :])
            facey[x] = face
            inner_y[x] = jnp.where(inside, face, 0.0)
            return carry

        lax.fori_loop(0, own_x + 1, face_x, 0)
        lax.fori_loop(0, own_x, face_y, 0)

    def lanes(c):
        return pl.ds(c * LANES, LANES)

    def ex_copy(side, c):
        if side < 2:
            src = sol.at[1 if side == 0 else own_x, pl.ds(8, own_y), lanes(c)]
            dst = sol.at[own_x + 1 if side == 0 else 0, pl.ds(8, own_y), lanes(c)]
            device = {"grp": g_dn if side == 0 else g_up}
        else:
            src = esend.at[side - 2, c]
            dst = erecv.at[side - 2, c]
            device = {"mem": m_dn if side == 2 else m_up}
        return pltpu.make_async_remote_copy(
            src_ref=src, dst_ref=dst, send_sem=ex_send.at[side], recv_sem=ex_recv.at[side, c],
            device_id=device, device_id_type=MESH,
        )

    def sol_rows(i, lifted):
        co = dot(bcor[i], lifted)
        for j in range(2):
            value = fine[2 * i + j, pl.ds(OV, own_y), :] + co[j * own_y : (j + 1) * own_y]
            sol[2 * i + j + 1, pl.ds(8, own_y), :] = value

    def correct_edges(lifted):
        co = dot(bedge[...].astype(BF16), lifted)
        low = fine[:, OV, :] + co[:own_x]
        high = fine[:, OV + own_y - 1, :] + co[own_x:]
        for c in range(chunks):
            esend[0, c] = low[:, c * LANES : (c + 1) * LANES]
            esend[1, c] = high[:, c * LANES : (c + 1) * LANES]
        sol_rows(0, lifted)
        sol_rows(own_x // 2 - 1, lifted)

    def ex_start():
        for c in range(chunks):
            for side in (2, 3, 0, 1):
                only((has_x + has_y)[side], ex_copy(side, c).start)

    def correct_inner(lifted):
        def step(i, carry):
            sol_rows(i, lifted)
            return carry

        lax.fori_loop(1, own_x // 2 - 1, step, 0, unroll=True)

    def zero_margin():
        zero = jnp.zeros((8, columns), F32)
        for x in range(own_x):
            sol[x + 1, pl.ds(0, 8), :] = zero
            sol[x + 1, pl.ds(own_y + 8, 8), :] = zero
            for it in range(2):
                res[it, x, pl.ds(0, 8), :] = zero
                res[it, x, pl.ds(own_y + 8, 8), :] = zero

    def thrice(v):
        return jnp.concatenate([v] * (columns // 128), axis=1)

    def inner_residual():
        def row(x, first, last):
            c = sol[x + 1, pl.ds(8, own_y), :]
            total = thrice(inner_y[x, pl.ds(1, own_y), :]) * (c - sol[x + 1, pl.ds(9, own_y), :])
            total += thrice(inner_y[x, pl.ds(0, own_y), :]) * (c - sol[x + 1, pl.ds(7, own_y), :])
            if not last:
                total += thrice(facex[x + 1]) * (c - sol[x + 2, pl.ds(8, own_y), :])
            if not first:
                total += thrice(facex[x]) * (c - sol[x, pl.ds(8, own_y), :])
            res[1, x, pl.ds(8, own_y), :] = res[0, x, pl.ds(8, own_y), :] - total

        def step(x, carry):
            row(x, False, False)
            return carry

        row(0, True, False)
        lax.fori_loop(1, own_x - 1, step, 0, unroll=2)
        row(own_x - 1, False, True)

    def rim_changes(c):
        for side in range(4):
            only((has_x + has_y)[side ^ 1], lambda side=side: ex_copy(side, c).wait_recv())
        low_x = jnp.where(g == 0, 0.0, sol[0, pl.ds(8, own_y), lanes(c)])
        high_x = jnp.where(g == n_grp - 1, 0.0, sol[own_x + 1, pl.ds(8, own_y), lanes(c)])
        low_x = facex[0] * (sol[1, pl.ds(8, own_y), lanes(c)] - low_x)
        high_x = facex[own_x] * (sol[own_x, pl.ds(8, own_y), lanes(c)] - high_x)
        low_y = facey[:, 0, :] * (esend[0, c] - jnp.where(m == 0, 0.0, erecv[1, c]))
        high_y = facey[:, own_y, :] * (esend[1, c] - jnp.where(m == n_mem - 1, 0.0, erecv[0, c]))
        return low_x, high_x, low_y, high_y

    def restrict_rim(c, total, low_x, high_x, low_y, high_y):
        zero = jnp.zeros_like(low_x)
        total = total - restrict_rows(bres[0], jnp.concatenate([low_x, zero], axis=0))
        total = total - restrict_rows(bres[own_x // 2 - 1], jnp.concatenate([zero, high_x], axis=0))
        total = total - restrict_rows(brim[...], jnp.concatenate([low_y, high_y], axis=0))
        rblk[1, c, own_rows, :] = total

    def rim_step(c, total):
        rim = rim_changes(c)
        restrict_rim(c, total[:, c * LANES : (c + 1) * LANES], *rim)
        gather_start(1, c)
        return rim

    def outer_residual(c, low_x, high_x, low_y, high_y):
        res[1, 0, pl.ds(8, own_y), lanes(c)] -= low_x
        res[1, own_x - 1, pl.ds(8, own_y), lanes(c)] -= high_x
        res[1, :, 8, lanes(c)] -= low_y
        res[1, :, own_y + 7, lanes(c)] -= high_y

    def finish_base():
        def step(x, carry):
            base_out[x] = sol[x + 1, pl.ds(8, own_y), :] + fine[x, pl.ds(OV, own_y), :]
            return carry

        lax.fori_loop(0, own_x, step, 0, unroll=2)

    blocks = mid // chunk
    restrict_rhs()
    load_cond.wait()
    pl.semaphore_wait(barrier, greets)
    for c in range(chunks):
        gather_start(0, c)
    cond_start()
    each_grp(lambda d: c_copy(d).start())
    c_local.start()
    prepare_basis()
    zero_margin()
    pack_x(0)
    pack_y(0)
    assemble(0)
    load_inv.wait()
    select_x()
    fine_inner(0, 3)
    gather_forward(0, 0, (1, 3, 2))
    gather_forward(0, 1, (1, 3, 2))
    gather_forward(0, 2, (1, 3, 2))
    x_start(0, True)
    x_start(0, False)
    corner_start(0)
    fine_inner(3, 4)
    y_start(0)
    fine_inner(4, blocks)
    make_faces()
    wait_bytes(cblk.at[pl.ds(0, (n_grp - 1) * modes), :], c_recv)
    c_local.wait()
    csplit[0], csplit[1] = split(cblk[...])
    coarse_step(0, 0)
    coarse_step(0, 1)
    select_y(0, 1)
    pair_step(0, 0)
    coarse_step(0, 2)
    pair_step(0, 1)
    select_y(1, 2)
    pair_step(0, 2)
    select_y(2, blocks)
    finish_y(0)
    finish_x(0)
    fine_outer(0)
    lifted = lift(0)
    correct_edges(lifted)
    ex_start()
    correct_inner(lifted)
    inner_residual()

    inner = restrict(1, 0, own_x // 2, jnp.zeros((modes, columns), F32))
    drain(0)
    rim_0 = rim_step(0, inner)
    rim_1 = rim_step(1, inner)
    rim_2 = rim_step(2, inner)
    outer_residual(0, *rim_0)
    outer_residual(1, *rim_1)
    outer_residual(2, *rim_2)
    pack_x(1)
    x_start(1, True)
    x_start(1, False)
    pack_y(1)
    corner_start(1)
    assemble(1)
    gather_forward(1, 0, (1, 3, 2))
    gather_forward(1, 1, (1, 3, 2))
    gather_forward(1, 2, (1, 3, 2))
    fine_inner(0, 2)
    y_start(1)
    fine_inner(2, 4)
    coarse_step(1, 0)
    coarse_step(1, 1)
    pair_step(1, 0)
    coarse_step(1, 2)
    pair_step(1, 1)
    fine_inner(4, 5)
    pair_step(1, 2)
    fine_inner(5, blocks)
    finish_y(1)
    finish_x(1)
    fine_outer(1)
    finish_base()
    drain(1)
    lifted_out[...] = lift(1)

    for side in range(4):
        sent = sol.at[1, pl.ds(8, own_y), :] if side < 2 else esend.at[side - 2]
        only((has_x + has_y)[side], lambda side=side, sent=sent: wait_bytes(sent, ex_send.at[side]))
    wait_bytes(sumbuf.at[1, :, pl.ds(1, n_pair - 1)], rs_send)


def tail_kernel(base, lifted, bcor, out_hbm, outbuf, out_sem):
    pairs, own_y = base.shape[0] // 2, base.shape[1]
    per = 2

    def store(i):
        rows = pl.ds(2 * per * i, 2 * per)
        return pltpu.make_async_copy(outbuf.at[rows], out_hbm.at[rows], out_sem.at[i])

    for i in range(pairs // per):
        for k in range(per * i, per * i + per):
            co = dot(bcor[k], lifted[...])
            for j in range(2):
                outbuf[2 * k + j] = base[2 * k + j] + co[j * own_y : (j + 1) * own_y]
        store(i).start()
    for i in range(pairs // per):
        store(i).wait()


def on_device(rhs, conductivity, local_inverse, coarse_basis, coarse_inverse):
    own_x, own_y, columns = rhs.shape
    modes = coarse_basis.shape[2]
    n_grp, n_mem = lax.axis_size("grp"), lax.axis_size("mem")
    n_y = n_mem // NZ
    chunks = columns // LANES
    span_x, span_y = own_x + 2 * OV, own_y + 2 * OV
    basis_t = jnp.transpose(coarse_basis, (0, 2, 1))
    arrays = (rhs, conductivity, local_inverse, basis_t, coarse_inverse)
    hbm = pl.BlockSpec(memory_space=pltpu.HBM)
    vmem = pl.BlockSpec(memory_space=pltpu.VMEM)
    dma = pltpu.SemaphoreType.DMA
    scratch = [
        pltpu.VMEM((own_x, own_y), F32),
        pltpu.VMEM((own_x, modes, own_y), F32),
        pltpu.VMEM((own_x * span_y, span_x * span_y), BF16),
        pltpu.VMEM((2, own_x, own_y + 16, columns), F32),
        pltpu.VMEM((own_x * span_y, columns), BF16),
        pltpu.VMEM((2, 2 * OV * (span_y + own_x), columns), BF16),
        pltpu.VMEM((own_x * span_y, 2 * OV * (span_y + own_x)), BF16),
        pltpu.VMEM((own_x * span_y, 2 * OV * own_x), BF16),
        pltpu.VMEM((own_x, span_y, columns), F32),
        pltpu.VMEM((own_x + 2, own_y + 16, columns), F32),
        pltpu.VMEM((own_x + 2, own_y + 16, 128), F32),
        pltpu.VMEM((own_x + 1, own_y, 128), F32),
        pltpu.VMEM((own_x, own_y + 8, 128), F32),
        pltpu.VMEM((own_x, own_y + 8, 128), F32),
        pltpu.VMEM((own_x // 2, 2 * modes, 2 * own_y), BF16),
        pltpu.VMEM((own_x // 2, 2 * own_y, 3 * modes), BF16),
        pltpu.VMEM((2 * own_x, 3 * modes), F32),
        pltpu.VMEM((2 * modes, 2 * own_x), BF16),
        pltpu.VMEM((2, chunks, n_mem * modes, LANES), F32),
        pltpu.VMEM((n_grp * modes, n_mem * modes), F32),
        pltpu.VMEM((2, n_grp * modes, n_mem * modes), BF16),
        pltpu.VMEM((2, chunks, n_grp // 2, 2, modes, LANES), F32),
        pltpu.VMEM((2, chunks, n_grp // 2, modes, LANES), F32),
        pltpu.VMEM((2, chunks, n_grp // 2, modes, LANES), F32),
        pltpu.VMEM((2, chunks, n_grp // 2, modes, LANES), F32),
        pltpu.VMEM((2, 2, own_x * OV, columns), BF16),
        pltpu.VMEM((2, 2, OV * own_y, columns), BF16),
        pltpu.VMEM((2, chunks, own_x, LANES), F32),
        pltpu.VMEM((2, chunks, own_x, LANES), F32),
        pltpu.VMEM((4, own_x, own_y), F32),
        dma((4,)), dma((3,)), dma,
        dma, dma, dma((4,)), dma((4,)),
        dma, dma((2, chunks, NZ - 1)), dma, dma((2, chunks)),
        dma((chunks,)), dma((2, chunks)), dma, dma((2, chunks)),
        dma((2,)), dma((2, 2)), dma((2,)), dma((2, 2)), dma((2, 2)), dma((2, 2, 2)),
        dma((4,)), dma((4, chunks)),
    ]
    base, lifted, bcor = pl.pallas_call(
        functools.partial(kernel, n_grp, n_mem, own_x, own_y),
        out_shape=(
            jax.ShapeDtypeStruct(rhs.shape, F32),
            jax.ShapeDtypeStruct((3 * modes, columns), BF16),
            jax.ShapeDtypeStruct((own_x // 2, 2 * own_y, 3 * modes), BF16),
        ),
        in_specs=[hbm] * 5,
        out_specs=(vmem, vmem, vmem),
        scratch_shapes=scratch,
        compiler_params=pltpu.CompilerParams(
            collective_id=0, has_side_effects=True, vmem_limit_bytes=44 * 1024 * 1024
        ),
    )(*(pltpu.with_memory_space_constraint(v, pltpu.HBM) for v in arrays))
    return pl.pallas_call(
        tail_kernel,
        out_shape=jax.ShapeDtypeStruct(rhs.shape, F32),
        in_specs=[vmem, vmem, vmem],
        out_specs=hbm,
        scratch_shapes=[pltpu.VMEM(rhs.shape, F32), dma((own_x // 4,))],
        compiler_params=pltpu.CompilerParams(vmem_limit_bytes=16 * 1024 * 1024),
    )(base, lifted, bcor)


def solution(mesh):
    placed = (
        P("grp", "mem", None),
        P("grp", "mem"),
        P(("grp", "mem"), None),
        P("grp", "mem", None),
        P(("grp", "mem"), None),
    )
    return jax.shard_map(
        on_device, mesh=mesh, in_specs=placed, out_specs=P("grp", "mem", None), check_vma=False
    )
```
